32 devices in a mesh: sec: 2 (over x), el: 16 (over z, y, core).
Axes of the slice: x: 2, y: 2, z: 4, core: 2. Of those that a mesh axis runs over, the one named last changes fastest.
Arguments:
- green_lesser: bfloat16 [2, 256, 64, 2, 128], P('sec', 'el'), may hold values from -6 to 6
- green_greater: bfloat16 [2, 256, 64, 2, 128], P('sec', 'el'), may hold values from -6 to 6
- coulomb: bfloat16 [2, 2, 256, 256], P('sec'), may hold values from -0.375 to 0.375
- pattern: int32 [2, 64], replicated, may hold values from 0 to 511, as said below
Outputs:
- polar: bfloat16 [2, 256, 64, 2, 128], P('sec', 'el')
- screened: bfloat16 [2, 256, 2, 256, 256], P('sec', 'el')
The draws below stay inside these ranges and needn't reach their ends.
Inputs may be any that keep to these rules, and one draw needn't show every extreme that they name: `pattern`: each row lists 64 distinct tile positions in increasing order.
All inputs are finite; a program needn't handle non-finite values.
Results may differ from the reference program's by a relative error of at most 0.014.
Values may be sent and summed in bfloat16 or wider, within the bound.
A program may use at most 128 MiB of HBM per device.

```python
import jax
import jax.numpy as jnp
from jax import lax

NB = 256
E = 256
TR = 8
TC = 16
TILE = 128
TILES = 512
NT = 64
RANGE = 32
CAP = 32
N_SEC = 2


def pattern_row(row_key):
    noise_key, owner_key = jax.random.split(row_key)
    positions = jnp.arange(TILES, dtype=jnp.int32)
    tile_row = positions // (NB // TC)
    tile_column = positions % (NB // TC)
    offset = jnp.abs(tile_row * TR - tile_column * TC)
    banded = jnp.where(offset < NB // 4, 1 << 19, 0).astype(jnp.int32)
    noise = jax.random.randint(noise_key, (TILES,), 0, 1 << 19, dtype=jnp.int32)
    chosen = jax.random.randint(owner_key, (), 0, TILES // RANGE, dtype=jnp.int32)
    forced = jnp.logical_and(positions // RANGE == chosen, positions % RANGE < CAP)
    score = (noise + banded + jnp.where(forced, 1 << 21, 0).astype(jnp.int32)) * TILES + positions
    best = lax.top_k(score, NT)[1]
    return jnp.sort(best).astype(jnp.int32)


def draw_pattern(key, part):
    keys = jax.random.split(jax.random.fold_in(key, 7), N_SEC)
    return jax.vmap(pattern_row)(keys)


def levels(rng, extent, cuts, low, top_value):
    def one(position, blocks):
        steps = jax.random.uniform(jax.random.fold_in(jax.random.fold_in(rng, 6), position), (blocks,), jnp.float32, low / len(cuts), top_value / len(cuts))
        return jnp.repeat(jnp.exp(steps), extent[position] // blocks).reshape((-1,) + (1,) * (len(extent) - position - 1))

    level = one(*cuts[0])
    for cut in cuts[1:]:
        level = level * one(*cut)
    return level


def bell_draw(rng, extent, spread, bound, cuts=(), kind=jnp.bfloat16):
    result = spread * jax.random.normal(rng, extent, jnp.float32)
    if cuts:
        result = result * levels(rng, extent, cuts, -0.22, 0.18)
    return jnp.clip(result, -bound, bound).astype(kind)


def setup_inputs(seed: int = 0) -> dict:
    streams_of = jax.random.split(jax.random.key(seed), 5)
    return {
        "green_lesser": bell_draw(streams_of[0], (N_SEC, E, NT, 2, TILE), 1.0, 6.0, ((0, 2), (1, 16))),
        "green_greater": bell_draw(streams_of[1], (N_SEC, E, NT, 2, TILE), 1.0, 6.0, ((0, 2), (1, 16))),
        "coulomb": bell_draw(streams_of[2], (N_SEC, 2, NB, NB), NB ** -0.5, 0.375, ((0, 2),)),
        "pattern": draw_pattern(jax.random.fold_in(streams_of[4], 71), 0),
    }


def correlate_section(lesser, greater):
    first = lesser[:, :, 0, :].astype(jnp.float32) + 1j * lesser[:, :, 1, :].astype(jnp.float32)
    second = greater[:, :, 0, :].astype(jnp.float32) + 1j * greater[:, :, 1, :].astype(jnp.float32)
    spectrum_first = jnp.fft.fft(first, n=2 * E, axis=0)
    spectrum_second = jnp.fft.fft(second, n=2 * E, axis=0)
    series = jnp.fft.ifft(spectrum_first * jnp.conj(spectrum_second), axis=0)[:E]
    factor = E ** -0.5
    return jnp.stack([-jnp.imag(series) * factor, jnp.real(series) * factor], axis=2).astype(jnp.bfloat16)


def to_block(tiles):
    count = tiles.shape[0]
    shaped = tiles.reshape(count, NB // TR, NB // TC, 2, TR, TC)
    return shaped.transpose(0, 3, 1, 4, 2, 5).reshape(count, 2, NB, NB)


def place(polar_section, listed):
    tiles = jnp.zeros((E, TILES, 2, TILE), jnp.bfloat16).at[:, listed].set(polar_section)
    return to_block(tiles)


def sandwich(matrix, blocks):
    wide = matrix.astype(jnp.float32)
    left = jnp.einsum('ij,ecjk->ecik', wide, blocks.astype(jnp.float32)).astype(jnp.bfloat16)
    return jnp.einsum('ecik,lk->ecil', left.astype(jnp.float32), wide)


def reference(green_lesser, green_greater, coulomb, pattern):
    polar = lax.map(lambda pair: correlate_section(pair[0], pair[1]), (green_lesser, green_greater))
    blocks = lax.map(lambda pair: place(pair[0], pair[1]), (polar, pattern))
    empty = jnp.zeros_like(blocks[:1])
    padded = jnp.concatenate([empty, blocks, empty], axis=0)
    upper = coulomb[:, 1]
    lower = jnp.concatenate([jnp.zeros_like(upper[:1]), upper[:-1]], axis=0)

    def screen(section):
        before = lax.dynamic_index_in_dim(padded, section, 0, keepdims=False)
        middle = lax.dynamic_index_in_dim(padded, section + 1, 0, keepdims=False)
        after = lax.dynamic_index_in_dim(padded, section + 2, 0, keepdims=False)
        diagonal = lax.dynamic_index_in_dim(coulomb[:, 0], section, 0, keepdims=False)
        forward = lax.dynamic_index_in_dim(upper, section, 0, keepdims=False)
        backward = lax.dynamic_index_in_dim(lower, section, 0, keepdims=False)
        total = sandwich(diagonal, middle) + sandwich(forward, after) + sandwich(backward.T, before)
        return total.astype(jnp.bfloat16)

    screened = lax.map(screen, jnp.arange(N_SEC, dtype=jnp.int32))
    return polar, screened
```

```python
import functools

import jax
import jax.numpy as jnp
import numpy as np
from jax import lax
from jax.experimental import pallas as pl
from jax.experimental.pallas import tpu as pltpu
from jax.sharding import PartitionSpec as P

TR = 8
TC = 16
VMEM_LIMIT = 56 * 1024 * 1024


def tables(energies):
    length = energies
    depth = energies // 2
    order = np.concatenate([np.arange(0, length, 2), np.arange(1, length, 2)])
    phase = np.outer(order, np.arange(depth)) % length
    phase = phase * (2.0 * np.pi / length)
    cosine = np.cos(phase).astype(np.float32)
    sine = np.sin(phase).astype(np.float32)
    real = np.stack([cosine, sine], axis=2).reshape(length, length)
    imag = np.stack([-sine, cosine], axis=2).reshape(length, length)
    forward = np.concatenate([real, imag], axis=0)
    out_r = np.concatenate([-sine.T, -cosine.T], axis=1)
    out_i = np.concatenate([cosine.T, -sine.T], axis=1)
    inverse = np.stack([out_r, out_i], axis=1).reshape(length, 2 * length)
    return jnp.asarray(forward, jnp.bfloat16), jnp.asarray(inverse, jnp.bfloat16)


def dot32(a, b):
    return jnp.dot(a, b, preferred_element_type=jnp.float32)


def conjugate_product(a, b):
    (ar, ai), (br, bi) = a, b
    return jnp.concatenate([ar * br + ai * bi, ai * br - ar * bi], axis=0).astype(jnp.bfloat16)


def spectra(parts, forward_ref):
    depth, _, width = parts[0].shape
    length = 2 * depth
    joined = jnp.concatenate([p.reshape(length, width) for p in parts], axis=1)
    z = dot32(forward_ref[...], joined)
    return [
        (z[:length, i * width : (i + 1) * width], z[length:, i * width : (i + 1) * width])
        for i in range(len(parts))
    ]


def low_part(factor, lesser, greater, forward_ref, inverse_ref):
    first, second = spectra([lesser, greater], forward_ref)
    return dot32(inverse_ref[...], conjugate_product(first, second)) * factor


def high_parts(factor, lesser, below, greater, forward_ref, inverse_ref):
    width = lesser.shape[-1]
    first, under, second = spectra([lesser, below, greater], forward_ref)
    middle = under[0].shape[0] // 2

    def shifted(a, b):
        return jnp.concatenate([b[:middle] + a[:middle], b[middle:] - a[middle:]], axis=0)

    both = tuple(shifted(a, b) for a, b in zip(under, second))
    product = jnp.concatenate(
        [conjugate_product(first, both), conjugate_product(first, under)], axis=1
    )
    series = dot32(inverse_ref[...], product) * factor
    return series[:, :width], series[:, width:]


def exchange_kernel(
    owners,
    sections,
    factor,
    lesser_ref,
    greater_ref,
    coulomb_ref,
    forward_ref,
    inverse_ref,
    *refs,
):
    sides = 1 if sections == 2 else 2
    polar_ref = refs[0]
    beside_refs = refs[1 : 1 + sides]
    other_ref = refs[1 + sides]
    (
        x_ref,
        below_ref,
        down_ref,
        partial_ref,
        d_ref,
        in_send,
        in_recv,
        pass_send,
        pass_recv,
        up_send,
        up_recv,
        down_send,
        down_recv,
        out_send,
        out_recv,
        side_send,
        side_recv,
        c_send,
        c_recv,
    ) = refs[2 + sides :]
    tiles = x_ref.shape[1]
    local = polar_ref.shape[0]
    width = polar_ref.shape[-1]
    group = owners // 4
    half = owners // 2
    me = lax.axis_index("el")
    section = lax.axis_index("sec")
    quarter = me // group
    place = lax.rem(me, group)
    base = quarter * group
    half_base = (quarter // 2) * half
    spot = lax.rem(me, half)
    mesh_id = pl.DeviceIdType.MESH
    if sections == 2:
        targets = [1 - section]
    else:
        targets = [
            lax.rem(section + 1, sections),
            lax.rem(section + sections - 1, sections),
        ]

    barrier = pltpu.get_barrier_semaphore()

    def greet(step, carry):
        peer = half_base + lax.rem(spot + step, half)
        pl.semaphore_signal(barrier, inc=1, device_id={"el": peer}, device_id_type=mesh_id)
        return carry

    lax.fori_loop(1, half, greet, 0)
    for target in targets:
        pl.semaphore_signal(barrier, inc=1, device_id={"sec": target}, device_id_type=mesh_id)

    def greet_across(peer):
        pl.semaphore_signal(barrier, inc=1, device_id={"el": peer}, device_id_type=mesh_id)
        pl.semaphore_wait(barrier, half + sides)

    @pl.when(quarter == 1)
    def _():
        greet_across(me + group)

    @pl.when(quarter == 2)
    def _():
        greet_across(me - group)

    @pl.when(jnp.logical_or(quarter == 0, quarter == 3))
    def _():
        pl.semaphore_wait(barrier, half - 1 + sides)

    mine = pl.ds(spot * local, local)
    own = pl.ds(lax.rem(quarter, 2) * group * local, group * local)
    theirs = pl.ds((1 - lax.rem(quarter, 2)) * group * local, group * local)

    def send_in(which, source, tile):
        pltpu.make_async_copy(
            source.at[:, place, tile], x_ref.at[which, tile, mine], in_recv.at[which, tile]
        ).start()

        def send(turn, carry):
            peer = lax.rem(place + 1 + turn, group)
            pltpu.make_async_remote_copy(
                src_ref=source.at[:, peer, tile],
                dst_ref=x_ref.at[which, tile, mine],
                send_sem=in_send,
                recv_sem=in_recv.at[which, tile],
                device_id={"el": base + peer},
                device_id_type=mesh_id,
            ).start()
            return carry

        lax.fori_loop(0, group - 1, send, 0)

    @pl.when(quarter < 2)
    def _():
        def send_g(tile, carry):
            send_in(1, greater_ref, tile)
            return carry

        def send_l(tile, carry):
            send_in(0, lesser_ref, tile)
            return carry

        lax.fori_loop(0, tiles, send_g, 0)
        lax.fori_loop(0, tiles, send_l, 0)

    @pl.when(quarter >= 2)
    def _():
        def send_both(tile, carry):
            send_in(0, lesser_ref, tile)
            send_in(1, greater_ref, tile)
            return carry

        lax.fori_loop(0, tiles, send_both, 0)

    shared = pltpu.make_async_remote_copy(
        src_ref=coulomb_ref.at[1],
        dst_ref=other_ref,
        send_sem=c_send,
        recv_sem=c_recv,
        device_id={"sec": targets[0]},
        device_id_type=mesh_id,
    )
    shared.start()

    def gathered(which, tile):
        part = x_ref.at[which, tile, own]
        pltpu.make_async_copy(part, part, in_recv.at[which, tile]).wait()

    def pass_inward(which, tile, peer):
        gathered(which, tile)
        pltpu.make_async_remote_copy(
            src_ref=x_ref.at[which, tile, own],
            dst_ref=x_ref.at[which, tile, own],
            send_sem=pass_send,
            recv_sem=pass_recv.at[which, tile],
            device_id={"el": peer},
            device_id_type=mesh_id,
        ).start()

    def passed(which, tile):
        part = x_ref.at[which, tile, theirs]
        pltpu.make_async_copy(part, part, pass_recv.at[which, tile]).wait()

    def forward_copy(tile, side):
        return pltpu.make_async_remote_copy(
            src_ref=polar_ref.at[:, :, tile],
            dst_ref=beside_refs[side].at[:, :, tile],
            send_sem=side_send.at[side, tile],
            recv_sem=side_recv.at[side, tile],
            device_id={"sec": targets[side]},
            device_id_type=mesh_id,
        )

    def pass_on(tile):
        whole = polar_ref.at[:, :, tile]
        pltpu.make_async_copy(whole, whole, out_recv.at[tile]).wait()
        for side in range(sides):
            forward_copy(tile, side).start()

    def give(tile):
        pltpu.make_async_copy(
            d_ref.at[tile, mine], polar_ref.at[:, place, tile], out_recv.at[tile]
        ).start()

        def send(turn, carry):
            peer = lax.rem(spot + 1 + turn, half)
            pltpu.make_async_remote_copy(
                src_ref=d_ref.at[tile, pl.ds(peer * local, local)],
                dst_ref=polar_ref.at[:, place, tile],
                send_sem=out_send,
                recv_sem=out_recv.at[tile],
                device_id={"el": half_base + peer},
                device_id_type=mesh_id,
            ).start()
            return carry

        lax.fori_loop(0, half - 1, send, 0)

    def outer(peer, pairs):
        for order in pairs:

            def step(tile, carry, order=order):
                for which in order:
                    pass_inward(which, tile, peer)
                return carry

            lax.fori_loop(0, tiles, step, 0)

        def finish(tile, carry):
            pass_on(tile)
            return carry

        lax.fori_loop(0, tiles, finish, 0)
        part = x_ref.at[:, :, own]
        pltpu.make_async_copy(part, part, pass_send).wait()

    @pl.when(quarter == 0)
    def _():
        outer(me + group, [(1,), (0,)])

    @pl.when(quarter == 3)
    def _():
        outer(me - group, [(0, 1)])

    def late(step):
        lag = 2

        def body(tile, carry):
            step(tile)

            @pl.when(tile >= lag)
            def _():
                pass_on(tile - lag)

            return carry

        lax.fori_loop(0, tiles, body, 0)
        for tile in range(max(tiles - lag, 0), tiles):
            pass_on(tile)
        sent = (half - 1) * local
        part = d_ref.at[:, pl.ds(0, sent)]
        pltpu.make_async_copy(part, part, out_send).wait()

    @pl.when(quarter == 1)
    def _():
        def lift(tile, carry):
            gathered(1, tile)
            passed(1, tile)
            pltpu.make_async_remote_copy(
                src_ref=x_ref.at[1, tile],
                dst_ref=below_ref.at[tile],
                send_sem=up_send,
                recv_sem=up_recv.at[tile],
                device_id={"el": me + group},
                device_id_type=mesh_id,
            ).start()
            return carry

        lax.fori_loop(0, tiles, lift, 0)

        def step(tile):
            gathered(0, tile)
            passed(0, tile)
            value = low_part(factor, x_ref[0, tile], x_ref[1, tile], forward_ref, inverse_ref)
            part = partial_ref.at[tile]
            pltpu.make_async_copy(part, part, down_recv.at[tile]).wait()
            value = value + partial_ref[tile].reshape(value.shape).astype(jnp.float32)
            d_ref[tile] = value.astype(jnp.bfloat16).reshape(d_ref.shape[1:])
            give(tile)

        late(step)
        pltpu.make_async_copy(below_ref, below_ref, up_send).wait()

    @pl.when(quarter == 2)
    def _():
        def step(tile):
            gathered(0, tile)
            gathered(1, tile)
            passed(0, tile)
            passed(1, tile)
            part = below_ref.at[tile]
            pltpu.make_async_copy(part, part, up_recv.at[tile]).wait()
            lower, upper = high_parts(
                factor, x_ref[0, tile], below_ref[tile], x_ref[1, tile], forward_ref, inverse_ref
            )
            shape = d_ref.shape[1:]
            down_ref[tile] = lower.astype(jnp.bfloat16).reshape(shape)
            pltpu.make_async_remote_copy(
                src_ref=down_ref.at[tile],
                dst_ref=partial_ref.at[tile],
                send_sem=down_send,
                recv_sem=down_recv.at[tile],
                device_id={"el": me - group},
                device_id_type=mesh_id,
            ).start()
            d_ref[tile] = upper.astype(jnp.bfloat16).reshape(shape)
            give(tile)

        late(step)
        pltpu.make_async_copy(down_ref, down_ref, down_send).wait()

    part = x_ref.at[:, :, pl.ds(0, (group - 1) * local)]
    pltpu.make_async_copy(part, part, in_send).wait()

    def settle(tile, carry):
        for side in range(sides):
            forward_copy(tile, side).wait()
        return carry

    lax.fori_loop(0, tiles, settle, 0)
    shared.wait()


def exchange(owners, sections, lesser, greater, coulomb):
    local, count, _, width = lesser.shape
    group = owners // 4
    tiles = count // group
    energies = local * owners
    depth = energies // 2
    sides = 1 if sections == 2 else 2
    forward, inverse = tables(energies)
    split = (local, group, tiles, 2, width)
    tile_shape = jax.ShapeDtypeStruct(split, jnp.bfloat16)
    anywhere = pl.BlockSpec(memory_space=pl.ANY)
    near = pl.BlockSpec(memory_space=pltpu.VMEM)
    dma = pltpu.SemaphoreType.DMA
    buffer = pltpu.VMEM((tiles, depth, 2, width), jnp.bfloat16)
    return pl.pallas_call(
        functools.partial(exchange_kernel, owners, sections, 1.0 / (energies * energies**0.5)),
        in_specs=[anywhere] * 3 + [near] * 2,
        out_specs=[near] * (2 + sides),
        out_shape=[tile_shape] * (1 + sides)
        + [jax.ShapeDtypeStruct(coulomb.shape[1:], coulomb.dtype)],
        scratch_shapes=[
            pltpu.VMEM((2, tiles, depth, 2, width), jnp.bfloat16),
            buffer,
            buffer,
            buffer,
            buffer,
            dma(()),
            dma((2, tiles)),
            dma(()),
            dma((2, tiles)),
            dma(()),
            dma((tiles,)),
            dma(()),
            dma((tiles,)),
            dma(()),
            dma((tiles,)),
            dma((sides, tiles)),
            dma((sides, tiles)),
            dma(()),
            dma(()),
        ],
        compiler_params=pltpu.CompilerParams(
            collective_id=0, has_side_effects=True, vmem_limit_bytes=VMEM_LIMIT
        ),
    )(lesser.reshape(split), greater.reshape(split), coulomb, forward, inverse)


def screen_setup(sections, coulomb_ref, other_ref, pattern_ref, right_ref, picked_ref, mask_ref):
    terms, count, nb = mask_ref.shape
    section = lax.axis_index("sec")
    lower = other_ref[...].astype(jnp.float32).T
    upper = coulomb_ref[1].astype(jnp.float32)
    matrices = [coulomb_ref[0].astype(jnp.float32)]
    if sections == 2:
        sources = [section, 1 - section]
        matrices.append(jnp.where(section == 0, upper, lower))
    else:
        sources = [
            section,
            lax.rem(section + sections - 1, sections),
            lax.rem(section + 1, sections),
        ]
        matrices.append(jnp.where(section > 0, lower, 0.0))
        matrices.append(jnp.where(section < sections - 1, upper, 0.0))
    position = lax.broadcasted_iota(jnp.int32, (nb, TR * count), 0)
    lane = lax.broadcasted_iota(jnp.int32, (count, nb), 1) // TC
    first = lax.broadcasted_iota(jnp.int32, (count, count), 0)
    second = lax.broadcasted_iota(jnp.int32, (count, count), 1)
    across = nb // TC
    for t in range(terms):
        listed = pattern_ref[pl.ds(sources[t], 1), :]
        row = jnp.concatenate([listed // across * TR + r for r in range(TR)], axis=1)
        chosen = jnp.where(position == row, 1.0, 0.0).astype(jnp.bfloat16)
        picked_ref[t] = dot32(matrices[t].astype(jnp.bfloat16), chosen).astype(jnp.bfloat16)
        column = jnp.sum(
            jnp.where(first == second, (listed % across).astype(jnp.float32), 0.0),
            axis=1,
            keepdims=True,
        ).astype(jnp.int32)
        mask_ref[t] = jnp.where(lane == column, 1.0, 0.0).astype(jnp.bfloat16)
        right_ref[t * nb : (t + 1) * nb] = matrices[t].T.astype(jnp.bfloat16)


def screen_kernel(sections, terms, batch, *refs):
    tile_refs = refs[:terms]
    coulomb_ref, other_ref, pattern_ref, out_ref = refs[terms : terms + 4]
    right_ref, picked_ref, mask_ref, rows_ref = refs[terms + 4 :]
    _, count, nb = mask_ref.shape
    width = rows_ref.shape[-1]

    @pl.when(pl.program_id(0) == 0)
    def _():
        screen_setup(
            sections, coulomb_ref, other_ref, pattern_ref, right_ref, picked_ref, mask_ref
        )

    lane = lax.broadcasted_iota(jnp.int32, (count, width), 1) % TC
    joined = [[] for _ in range(batch * 2)]
    for t in range(terms):
        for b in range(batch):
            rows_ref[t, b] = tile_refs[t][b].reshape(2 * count, width).astype(jnp.float32)
        mask = mask_ref[t]
        for b in range(batch):
            for c in range(2):
                tile = rows_ref[t, b, pl.ds(c, count, stride=2), :]
                pieces = []
                for r in range(TR):
                    spread = jnp.take_along_axis(
                        tile, lane + r * TC, axis=1, mode="promise_in_bounds"
                    )
                    spread = spread.astype(jnp.bfloat16)
                    wide = jnp.concatenate([spread] * (nb // width), axis=1)
                    pieces.append(wide * mask)
                stacked = jnp.concatenate(pieces, axis=0)
                joined[2 * b + c].append(dot32(picked_ref[t], stacked).astype(jnp.bfloat16))
    left = jnp.concatenate([jnp.concatenate(j, axis=1) for j in joined], axis=0)
    total = dot32(left, right_ref[...]).astype(jnp.bfloat16)
    out_ref[...] = total.reshape(batch, 2, nb, nb)


def screen(sections, tiles, coulomb, other, pattern):
    terms = len(tiles)
    energies, owners, slots, _, width = tiles[0].shape
    count = owners * slots
    nb = coulomb.shape[1]
    batch = next(n for n in (8, 4, 2, 1) if energies % n == 0)
    whole = lambda array: pl.BlockSpec(array.shape, lambda i: (0,) * array.ndim)
    return pl.pallas_call(
        functools.partial(screen_kernel, sections, terms, batch),
        grid=(energies // batch,),
        in_specs=[pl.BlockSpec((batch, owners, slots, 2, width), lambda i: (i, 0, 0, 0, 0))] * terms
        + [whole(coulomb), whole(other), whole(pattern)],
        out_specs=pl.BlockSpec((batch, 2, nb, nb), lambda i: (i, 0, 0, 0)),
        out_shape=jax.ShapeDtypeStruct((energies, 2, nb, nb), jnp.bfloat16),
        scratch_shapes=[
            pltpu.VMEM((terms * nb, nb), jnp.bfloat16),
            pltpu.VMEM((terms, nb, TR * count), jnp.bfloat16),
            pltpu.VMEM((terms, count, nb), jnp.bfloat16),
            pltpu.VMEM((terms, batch, 2 * count, width), jnp.float32),
        ],
        compiler_params=pltpu.CompilerParams(vmem_limit_bytes=VMEM_LIMIT),
    )(*tiles, coulomb, other, pattern)


def on_device(sections, owners, green_lesser, green_greater, coulomb, pattern):
    _, local, count, _, width = green_lesser.shape
    polar, *beside, other = exchange(
        owners, sections, green_lesser[0], green_greater[0], coulomb[0]
    )
    screened = screen(sections, [polar, *beside], coulomb[0], other, pattern)
    return polar.reshape(1, local, count, 2, width), screened[None]


def solution(mesh):
    in_specs = (
        P("sec", "el", None, None, None),
        P("sec", "el", None, None, None),
        P("sec", None, None, None),
        P(),
    )
    out_specs = (P("sec", "el", None, None, None), P("sec", "el", None, None, None))
    return jax.shard_map(
        functools.partial(on_device, mesh.shape["sec"], mesh.shape["el"]),
        mesh=mesh,
        in_specs=in_specs,
        out_specs=out_specs,
        check_vma=False,
    )
```

```python
import functools

import jax
import jax.numpy as jnp
import numpy as np
from jax import lax
from jax.experimental import pallas as pl
from jax.experimental.pallas import tpu as pltpu
from jax.sharding import PartitionSpec as P

TR = 8
TC = 16
VMEM_LIMIT = 56 * 1024 * 1024
GROUPS = 4
BATCHES = 4


def tables(energies):
    length = energies
    depth = energies // 2
    order = np.concatenate([np.arange(0, length, 2), np.arange(1, length, 2)])
    phase = np.outer(order, np.arange(depth)) % length
    phase = phase * (2.0 * np.pi / length)
    cosine = np.cos(phase).astype(np.float32)
    sine = np.sin(phase).astype(np.float32)
    real = np.stack([cosine, sine], axis=2).reshape(length, length)
    imag = np.stack([-sine, cosine], axis=2).reshape(length, length)
    forward = np.concatenate([real, imag], axis=0)
    out_r = np.concatenate([-sine.T, -cosine.T], axis=1)
    out_i = np.concatenate([cosine.T, -sine.T], axis=1)
    inverse = np.stack([out_r, out_i], axis=1).reshape(length, 2 * length)
    return jnp.asarray(forward, jnp.bfloat16), jnp.asarray(inverse, jnp.bfloat16)


def dot32(a, b):
    return jnp.dot(a, b, preferred_element_type=jnp.float32)


def conjugate_product(a, b):
    (ar, ai), (br, bi) = a, b
    return jnp.concatenate([ar * br + ai * bi, ai * br - ar * bi], axis=0).astype(jnp.bfloat16)


def spectra(parts, forward_ref):
    depth, _, width = parts[0].shape
    length = 2 * depth
    joined = jnp.concatenate([p.reshape(length, width) for p in parts], axis=1)
    z = dot32(forward_ref[...], joined)
    return [
        (z[:length, i * width : (i + 1) * width], z[length:, i * width : (i + 1) * width])
        for i in range(len(parts))
    ]


def low_part(factor, lesser, greater, forward_ref, inverse_ref):
    first, second = spectra([lesser, greater], forward_ref)
    return dot32(inverse_ref[...], conjugate_product(first, second)) * factor


def high_parts(factor, lesser, below, greater, forward_ref, inverse_ref):
    width = lesser.shape[-1]
    first, under, second = spectra([lesser, below, greater], forward_ref)
    middle = under[0].shape[0] // 2

    def shifted(a, b):
        return jnp.concatenate([b[:middle] + a[:middle], b[middle:] - a[middle:]], axis=0)

    both = tuple(shifted(a, b) for a, b in zip(under, second))
    product = jnp.concatenate(
        [conjugate_product(first, both), conjugate_product(first, under)], axis=1
    )
    series = dot32(inverse_ref[...], product) * factor
    return series[:, :width], series[:, width:]


def exchange_kernel(
    owners,
    sections,
    factor,
    lesser_ref,
    greater_ref,
    coulomb_ref,
    forward_ref,
    inverse_ref,
    pattern_ref,
    *refs,
):
    sides = 1 if sections == 2 else 2
    polar_ref = refs[0]
    beside_refs = refs[1 : 1 + sides]
    sum_hbm, right_ref, picked_last_ref, mask_last_ref = refs[1 + sides : 5 + sides]
    (
        other_ref,
        coulomb_near,
        sum_ref,
        picked_ref,
        mask_ref,
        rows_ref,
        low_ref,
        sum_sem,
        near_sem,
        x_ref,
        below_ref,
        down_ref,
        partial_ref,
        d_ref,
        in_send,
        in_recv,
        pass_send,
        pass_recv,
        up_send,
        up_recv,
        down_send,
        down_recv,
        out_send,
        out_recv,
        side_send,
        side_recv,
        c_send,
        c_recv,
    ) = refs[5 + sides :]
    tiles = x_ref.shape[1]
    local = polar_ref.shape[0]
    slots = tiles // GROUPS
    some = local // BATCHES
    group = owners // 4
    half = owners // 2
    me = lax.axis_index("el")
    section = lax.axis_index("sec")
    quarter = me // group
    place = lax.rem(me, group)
    base = quarter * group
    half_base = (quarter // 2) * half
    spot = lax.rem(me, half)
    outer = jnp.logical_or(quarter == 0, quarter == 3)
    inward = jnp.where(quarter == 0, me + group, me - group)
    mesh_id = pl.DeviceIdType.MESH
    if sections == 2:
        targets = [1 - section]
    else:
        targets = [
            lax.rem(section + 1, sections),
            lax.rem(section + sections - 1, sections),
        ]

    barrier = pltpu.get_barrier_semaphore()

    def greet(step, carry):
        peer = half_base + lax.rem(spot + step, half)
        pl.semaphore_signal(barrier, inc=1, device_id={"el": peer}, device_id_type=mesh_id)
        return carry

    lax.fori_loop(1, half, greet, 0)
    for target in targets:
        pl.semaphore_signal(barrier, inc=1, device_id={"sec": target}, device_id_type=mesh_id)

    def greet_across(peer):
        pl.semaphore_signal(barrier, inc=1, device_id={"el": peer}, device_id_type=mesh_id)
        pl.semaphore_wait(barrier, half + sides)

    @pl.when(quarter == 1)
    def _():
        greet_across(me + group)

    @pl.when(quarter == 2)
    def _():
        greet_across(me - group)

    @pl.when(outer)
    def _():
        pl.semaphore_wait(barrier, half - 1 + sides)

    mine = pl.ds(spot * local, local)
    own = pl.ds(lax.rem(quarter, 2) * group * local, group * local)
    theirs = pl.ds((1 - lax.rem(quarter, 2)) * group * local, group * local)

    def send_in(which, source, tile):
        pltpu.make_async_copy(
            source.at[:, place, tile], x_ref.at[which, tile, mine], in_recv.at[which, tile]
        ).start()

        def send(turn, carry):
            peer = lax.rem(place + 1 + turn, group)
            pltpu.make_async_remote_copy(
                src_ref=source.at[:, peer, tile],
                dst_ref=x_ref.at[which, tile, mine],
                send_sem=in_send,
                recv_sem=in_recv.at[which, tile],
                device_id={"el": base + peer},
                device_id_type=mesh_id,
            ).start()
            return carry

        lax.fori_loop(0, group - 1, send, 0)

    def send_both(tile, carry):
        send_in(1, greater_ref, tile)
        send_in(0, lesser_ref, tile)
        return carry

    lax.fori_loop(0, tiles, send_both, 0)

    shared = pltpu.make_async_remote_copy(
        src_ref=coulomb_ref.at[1],
        dst_ref=other_ref,
        send_sem=c_send,
        recv_sem=c_recv,
        device_id={"sec": targets[0]},
        device_id_type=mesh_id,
    )
    shared.start()

    def gathered(which, tile):
        part = x_ref.at[which, tile, own]
        pltpu.make_async_copy(part, part, in_recv.at[which, tile]).wait()

    def pass_inward(which, tile, peer):
        gathered(which, tile)
        pltpu.make_async_remote_copy(
            src_ref=x_ref.at[which, tile, own],
            dst_ref=x_ref.at[which, tile, own],
            send_sem=pass_send,
            recv_sem=pass_recv.at[which, tile],
            device_id={"el": peer},
            device_id_type=mesh_id,
        ).start()

    def passed(which, tile):
        part = x_ref.at[which, tile, theirs]
        pltpu.make_async_copy(part, part, pass_recv.at[which, tile]).wait()

    def forward_copy(tile, side):
        return pltpu.make_async_remote_copy(
            src_ref=polar_ref.at[:, :, tile],
            dst_ref=beside_refs[side].at[:, :, tile],
            send_sem=side_send.at[side, tile],
            recv_sem=side_recv.at[side, tile],
            device_id={"sec": targets[side]},
            device_id_type=mesh_id,
        )

    def pass_on(tile):
        whole = polar_ref.at[:, :, tile]
        pltpu.make_async_copy(whole, whole, out_recv.at[tile]).wait()
        for side in range(sides):
            forward_copy(tile, side).start()

    def give(tile):
        pltpu.make_async_copy(
            d_ref.at[tile, mine], polar_ref.at[:, place, tile], out_recv.at[tile]
        ).start()

        def send(turn, carry):
            peer = lax.rem(spot + 1 + turn, half)
            pltpu.make_async_remote_copy(
                src_ref=d_ref.at[tile, pl.ds(peer * local, local)],
                dst_ref=polar_ref.at[:, place, tile],
                send_sem=out_send,
                recv_sem=out_recv.at[tile],
                device_id={"el": half_base + peer},
                device_id_type=mesh_id,
            ).start()
            return carry

        lax.fori_loop(0, half - 1, send, 0)

    def lift(tile):
        gathered(1, tile)
        passed(1, tile)
        pltpu.make_async_remote_copy(
            src_ref=x_ref.at[1, tile],
            dst_ref=below_ref.at[tile],
            send_sem=up_send,
            recv_sem=up_recv.at[tile],
            device_id={"el": me + group},
            device_id_type=mesh_id,
        ).start()
        gathered(0, tile)
        passed(0, tile)
        low_ref[tile] = low_part(factor, x_ref[0, tile], x_ref[1, tile], forward_ref, inverse_ref)

    def complete(tile):
        part = partial_ref.at[tile]
        pltpu.make_async_copy(part, part, down_recv.at[tile]).wait()
        value = low_ref[tile]
        value = value + partial_ref[tile].reshape(value.shape).astype(jnp.float32)
        d_ref[tile] = value.astype(jnp.bfloat16).reshape(d_ref.shape[1:])
        give(tile)

    def upper(tile):
        gathered(0, tile)
        gathered(1, tile)
        passed(0, tile)
        passed(1, tile)
        part = below_ref.at[tile]
        pltpu.make_async_copy(part, part, up_recv.at[tile]).wait()
        down, above = high_parts(
            factor, x_ref[0, tile], below_ref[tile], x_ref[1, tile], forward_ref, inverse_ref
        )
        shape = d_ref.shape[1:]
        down_ref[tile] = down.astype(jnp.bfloat16).reshape(shape)
        pltpu.make_async_remote_copy(
            src_ref=down_ref.at[tile],
            dst_ref=partial_ref.at[tile],
            send_sem=down_send,
            recv_sem=down_recv.at[tile],
            device_id={"el": me - group},
            device_id_type=mesh_id,
        ).start()
        d_ref[tile] = above.astype(jnp.bfloat16).reshape(shape)
        give(tile)

    def prepare():
        pltpu.make_async_copy(coulomb_ref, coulomb_near, near_sem).wait()
        shared.wait_recv()
        screen_setup(
            sections,
            coulomb_near,
            other_ref,
            pattern_ref,
            right_ref,
            picked_ref,
            mask_ref,
            tiles,
        )
        picked_last_ref[...] = picked_ref[GROUPS - 1]
        mask_last_ref[...] = mask_ref[GROUPS - 1]
        for b in range(local):
            sum_ref[b] = jnp.zeros(sum_ref.shape[1:], sum_ref.dtype)

    def sum_copy(batch):
        part = pl.ds(batch * some, some)
        return pltpu.make_async_copy(sum_ref.at[part], sum_hbm.at[part], sum_sem.at[batch])

    def screen_some(turn):
        chunk = turn // BATCHES
        batch = lax.rem(turn, BATCHES)

        @pl.when(batch == 0)
        def _():
            for s in range(slots):
                for side in range(sides):
                    forward_copy(chunk * slots + s, side).wait_recv()

        start = batch * some
        columns = pl.ds(chunk * slots, slots)
        sources = [polar_ref, *beside_refs]
        for t in range(1 + sides):
            for b in range(some):
                piece = sources[t][start + b, :, columns]
                rows_ref[t, b] = piece.reshape(rows_ref.shape[2:]).astype(jnp.float32)
        masks = [mask_ref[chunk, t] for t in range(1 + sides)]
        added = screen_chunk(some, rows_ref, masks, right_ref, picked_ref[chunk])
        for b in range(some):
            for c in range(2):
                old = sum_ref[start + b, c].astype(jnp.float32)
                sum_ref[start + b, c] = (old + added[2 * b + c]).astype(jnp.bfloat16)

        @pl.when(chunk == GROUPS - 2)
        def _():
            sum_copy(batch).start()

    pltpu.make_async_copy(coulomb_ref, coulomb_near, near_sem).start()
    turns = (GROUPS - 1) * BATCHES
    lead = slots + 2
    last = max(tiles, turns + lead)
    behind = 6
    delay = jnp.where(outer, tiles, jnp.where(quarter == 1, behind + 2, 2))
    ready = jnp.where(outer, tiles, jnp.where(quarter == 1, 3, 0))

    def body(i, carry):
        @pl.when(jnp.logical_and(outer, i < tiles))
        def _():
            pass_inward(1, i, inward)
            pass_inward(0, i, inward)

        @pl.when(jnp.logical_and(quarter == 1, i < tiles))
        def _():
            lift(i)

        @pl.when(i == ready)
        def _():
            prepare()

        @pl.when(
            jnp.logical_and(quarter == 1, jnp.logical_and(i >= behind, i < tiles + behind))
        )
        def _():
            complete(i - behind)

        @pl.when(jnp.logical_and(quarter == 2, i < tiles))
        def _():
            upper(i)

        tile = i - delay

        @pl.when(jnp.logical_and(tile >= 0, tile < tiles))
        def _():
            pass_on(tile)

        turn = tile - lead

        @pl.when(jnp.logical_and(turn >= 0, turn < turns))
        def _():
            screen_some(turn)

        return carry

    lax.fori_loop(0, last + delay, body, 0)

    @pl.when(outer)
    def _():
        part = x_ref.at[:, :, own]
        pltpu.make_async_copy(part, part, pass_send).wait()

    @pl.when(jnp.logical_not(outer))
    def _():
        part = d_ref.at[:, pl.ds(0, (half - 1) * local)]
        pltpu.make_async_copy(part, part, out_send).wait()

    @pl.when(quarter == 1)
    def _():
        pltpu.make_async_copy(below_ref, below_ref, up_send).wait()

    @pl.when(quarter == 2)
    def _():
        pltpu.make_async_copy(down_ref, down_ref, down_send).wait()

    part = x_ref.at[:, :, pl.ds(0, (group - 1) * local)]
    pltpu.make_async_copy(part, part, in_send).wait()
    for batch in range(BATCHES):
        sum_copy(batch).wait()

    def settle_sent(tile, carry):
        for side in range(sides):
            forward_copy(tile, side).wait_send()
        return carry

    def settle(tile, carry):
        for side in range(sides):
            forward_copy(tile, side).wait()
        return carry

    lax.fori_loop(0, (GROUPS - 1) * slots, settle_sent, 0)
    lax.fori_loop((GROUPS - 1) * slots, tiles, settle, 0)
    shared.wait_send()


def exchange(owners, sections, lesser, greater, coulomb, pattern):
    local, count, _, width = lesser.shape
    group = owners // 4
    tiles = count // group
    energies = local * owners
    depth = energies // 2
    nb = coulomb.shape[1]
    sides = 1 if sections == 2 else 2
    terms = 1 + sides
    chunk = count // GROUPS
    forward, inverse = tables(energies)
    split = (local, group, tiles, 2, width)
    bf16 = jnp.bfloat16
    tile_shape = jax.ShapeDtypeStruct(split, bf16)
    anywhere = pl.BlockSpec(memory_space=pl.ANY)
    near = pl.BlockSpec(memory_space=pltpu.VMEM)
    dma = pltpu.SemaphoreType.DMA
    buffer = pltpu.VMEM((tiles, depth, 2, width), bf16)
    return pl.pallas_call(
        functools.partial(exchange_kernel, owners, sections, 1.0 / (energies * energies**0.5)),
        in_specs=[anywhere] * 3 + [near] * 3,
        out_specs=[near] * (1 + sides) + [anywhere] + [near] * 3,
        out_shape=[tile_shape] * (1 + sides)
        + [
            jax.ShapeDtypeStruct((local, 2, nb, nb), bf16),
            jax.ShapeDtypeStruct((terms, nb, nb), bf16),
            jax.ShapeDtypeStruct((nb, terms * TR * chunk), bf16),
            jax.ShapeDtypeStruct((terms, chunk, nb), bf16),
        ],
        scratch_shapes=[
            pltpu.VMEM((nb, nb), bf16),
            pltpu.VMEM(coulomb.shape, bf16),
            pltpu.VMEM((local, 2, nb, nb), bf16),
            pltpu.VMEM((GROUPS, nb, terms * TR * chunk), bf16),
            pltpu.VMEM((GROUPS, terms, chunk, nb), bf16),
            pltpu.VMEM((terms, local // BATCHES, 2 * chunk, width), jnp.float32),
            pltpu.VMEM((tiles, energies, width), jnp.float32),
            dma((BATCHES,)),
            dma(()),
            pltpu.VMEM((2, tiles, depth, 2, width), bf16),
            buffer,
            buffer,
            buffer,
            buffer,
            dma(()),
            dma((2, tiles)),
            dma(()),
            dma((2, tiles)),
            dma(()),
            dma((tiles,)),
            dma(()),
            dma((tiles,)),
            dma(()),
            dma((tiles,)),
            dma((sides, tiles)),
            dma((sides, tiles)),
            dma(()),
            dma(()),
        ],
        compiler_params=pltpu.CompilerParams(
            collective_id=0, has_side_effects=True, vmem_limit_bytes=VMEM_LIMIT
        ),
    )(lesser.reshape(split), greater.reshape(split), coulomb, forward, inverse, pattern)


def screen_setup(
    sections, coulomb_ref, other_ref, pattern_ref, right_ref, picked_ref, mask_ref, tiles
):
    groups, terms, chunk, nb = mask_ref.shape
    count = groups * chunk
    slots = tiles // groups
    section = lax.axis_index("sec")
    lower = other_ref[...].astype(jnp.float32).T
    upper = coulomb_ref[1].astype(jnp.float32)
    matrices = [coulomb_ref[0].astype(jnp.float32)]
    if sections == 2:
        sources = [section, 1 - section]
        matrices.append(jnp.where(section == 0, upper, lower))
    else:
        sources = [
            section,
            lax.rem(section + sections - 1, sections),
            lax.rem(section + 1, sections),
        ]
        matrices.append(jnp.where(section > 0, lower, 0.0))
        matrices.append(jnp.where(section < sections - 1, upper, 0.0))
    across = nb // TC
    wide = TR * count
    iota = lambda shape, axis: lax.broadcasted_iota(jnp.int32, shape, axis)
    row_of = iota((nb, wide), 0)
    lane = iota((count, wide), 1)
    member = lane % chunk
    listed_at = (member // slots) * tiles + lane // (TR * chunk) * slots + member % slots
    taken = listed_at == iota((count, wide), 0)
    inner_row = iota((1, wide), 1) // chunk % TR
    diagonal = iota((count, count), 0) == iota((count, count), 1)
    member = iota((chunk, count), 0)
    begin = (member // slots) * tiles + member % slots
    column_of = iota((chunk, nb), 1) // TC
    for t in range(terms):
        listed = pattern_ref[pl.ds(sources[t], 1), :].astype(jnp.float32)
        upright = jnp.sum(jnp.where(diagonal, listed, 0.0), axis=1, keepdims=True)
        spread = jnp.sum(jnp.where(taken, upright, 0.0), axis=0, keepdims=True).astype(jnp.int32)
        row = spread // across * TR + inner_row
        chosen = jnp.where(row_of == row, 1.0, 0.0).astype(jnp.bfloat16)
        picked = dot32(matrices[t].astype(jnp.bfloat16), chosen).astype(jnp.bfloat16)
        span = TR * chunk
        for g in range(groups):
            picked_ref[g, :, t * span : (t + 1) * span] = picked[:, g * span : (g + 1) * span]
            here = iota((chunk, count), 1) == begin + g * slots
            place = jnp.sum(jnp.where(here, listed, 0.0), axis=1, keepdims=True).astype(jnp.int32)
            mask_ref[g, t] = jnp.where(column_of == place % across, 1.0, 0.0).astype(jnp.bfloat16)
        right_ref[t] = matrices[t].T.astype(jnp.bfloat16)


def screen_chunk(batch, rows_ref, masks, right_ref, picked):
    terms = len(masks)
    chunk, nb = masks[0].shape
    width = rows_ref.shape[-1]
    lane = lax.broadcasted_iota(jnp.int32, (chunk, width), 1) % TC
    halves = []
    for t in range(terms):
        stacked = []
        for b in range(batch):
            for c in range(2):
                tile = rows_ref[t, b, pl.ds(c, chunk, stride=2), :]
                for r in range(TR):
                    spread = jnp.take_along_axis(
                        tile, lane + r * TC, axis=1, mode="promise_in_bounds"
                    ).astype(jnp.bfloat16)
                    stacked.append(jnp.concatenate([spread] * (nb // width), axis=1) * masks[t])
        stacked = jnp.concatenate(stacked, axis=0)
        halves.append(dot32(stacked, right_ref[t]).astype(jnp.bfloat16))
    span = TR * chunk
    added = []
    for n in range(2 * batch):
        part = jnp.concatenate([h[n * span : (n + 1) * span] for h in halves], axis=0)
        added.append(dot32(picked, part))
    return added


def screen_kernel(terms, batch, *refs):
    tile_refs = refs[:terms]
    polar_ref, sum_ref, right_ref, picked_ref, mask_ref = refs[terms : terms + 5]
    polar_out, out_ref, rows_ref = refs[terms + 5 :]
    polar_out[...] = polar_ref[...]
    for t in range(terms):
        for b in range(batch):
            rows_ref[t, b] = tile_refs[t][b].reshape(rows_ref.shape[2:]).astype(jnp.float32)
    masks = [mask_ref[t] for t in range(terms)]
    added = screen_chunk(batch, rows_ref, masks, right_ref, picked_ref[...])
    for b in range(batch):
        for c in range(2):
            out_ref[b, c] = (sum_ref[b, c].astype(jnp.float32) + added[2 * b + c]).astype(
                jnp.bfloat16
            )


def screen(tiles, total, right, picked, mask):
    terms = len(tiles)
    local, group, per, _, width = tiles[0].shape
    chunk, nb = mask.shape[1:]
    batch = local // BATCHES
    slots = per // GROUPS
    whole = lambda array: pl.BlockSpec(array.shape, lambda i: (0,) * array.ndim)
    some = pl.BlockSpec((batch, group, slots, 2, width), lambda i: (i, 0, GROUPS - 1, 0, 0))
    full = pl.BlockSpec((batch, group, per, 2, width), lambda i: (i, 0, 0, 0, 0))
    square = pl.BlockSpec((batch, 2, nb, nb), lambda i: (i, 0, 0, 0))
    return pl.pallas_call(
        functools.partial(screen_kernel, terms, batch),
        grid=(BATCHES,),
        in_specs=[some] * terms + [full, square, whole(right), whole(picked), whole(mask)],
        out_specs=[full, square],
        out_shape=[
            jax.ShapeDtypeStruct(tiles[0].shape, jnp.bfloat16),
            jax.ShapeDtypeStruct(total.shape, jnp.bfloat16),
        ],
        scratch_shapes=[pltpu.VMEM((terms, batch, 2 * chunk, width), jnp.float32)],
        compiler_params=pltpu.CompilerParams(vmem_limit_bytes=VMEM_LIMIT),
    )(*tiles, tiles[0], total, right, picked, mask)


def on_device(sections, owners, green_lesser, green_greater, coulomb, pattern):
    _, local, count, _, width = green_lesser.shape
    sides = 1 if sections == 2 else 2
    results = exchange(
        owners, sections, green_lesser[0], green_greater[0], coulomb[0], pattern
    )
    polar, screened = screen(results[: 1 + sides], *results[1 + sides :])
    return polar.reshape(1, local, count, 2, width), screened[None]


def solution(mesh):
    in_specs = (
        P("sec", "el", None, None, None),
        P("sec", "el", None, None, None),
        P("sec", None, None, None),
        P(),
    )
    out_specs = (P("sec", "el", None, None, None), P("sec", "el", None, None, None))
    return jax.shard_map(
        functools.partial(on_device, mesh.shape["sec"], mesh.shape["el"]),
        mesh=mesh,
        in_specs=in_specs,
        out_specs=out_specs,
        check_vma=False,
    )
```

```python
import functools

import jax
import jax.numpy as jnp
import numpy as np
from jax import lax
from jax.experimental import pallas as pl
from jax.experimental.pallas import tpu as pltpu
from jax.sharding import PartitionSpec as P

TR = 8
TC = 16
VMEM_LIMIT = 56 * 1024 * 1024
GROUPS = 4
BATCHES = 2


def tables(energies):
    length = energies
    depth = energies // 2
    order = np.concatenate([np.arange(0, length, 2), np.arange(1, length, 2)])
    phase = np.outer(order, np.arange(depth)) % length
    phase = phase * (2.0 * np.pi / length)
    cosine = np.cos(phase).astype(np.float32)
    sine = np.sin(phase).astype(np.float32)
    real = np.stack([cosine, sine], axis=2).reshape(length, length)
    imag = np.stack([-sine, cosine], axis=2).reshape(length, length)
    forward = np.concatenate([real, imag], axis=0)
    out_r = np.concatenate([-sine.T, -cosine.T], axis=1)
    out_i = np.concatenate([cosine.T, -sine.T], axis=1)
    inverse = np.stack([out_r, out_i], axis=1).reshape(length, 2 * length)
    return jnp.asarray(forward, jnp.bfloat16), jnp.asarray(inverse, jnp.bfloat16)


def dot32(a, b):
    return jnp.dot(a, b, preferred_element_type=jnp.float32)


def conjugate_product(a, b):
    (ar, ai), (br, bi) = a, b
    return jnp.concatenate([ar * br + ai * bi, ai * br - ar * bi], axis=0).astype(jnp.bfloat16)


def spectra(parts, forward_ref):
    depth, _, width = parts[0].shape
    length = 2 * depth
    joined = jnp.concatenate([p.reshape(length, width) for p in parts], axis=1)
    z = dot32(forward_ref[...], joined)
    return [
        (z[:length, i * width : (i + 1) * width], z[length:, i * width : (i + 1) * width])
        for i in range(len(parts))
    ]


def low_part(factor, lesser, greater, forward_ref, inverse_ref):
    first, second = spectra([lesser, greater], forward_ref)
    return dot32(inverse_ref[...], conjugate_product(first, second)) * factor


def high_parts(factor, lesser, below, greater, forward_ref, inverse_ref):
    width = lesser.shape[-1]
    first, under, second = spectra([lesser, below, greater], forward_ref)
    middle = under[0].shape[0] // 2

    def shifted(a, b):
        return jnp.concatenate([b[:middle] + a[:middle], b[middle:] - a[middle:]], axis=0)

    both = tuple(shifted(a, b) for a, b in zip(under, second))
    product = jnp.concatenate(
        [conjugate_product(first, both), conjugate_product(first, under)], axis=1
    )
    series = dot32(inverse_ref[...], product) * factor
    return series[:, :width], series[:, width:]


def exchange_kernel(
    owners,
    sections,
    factor,
    lesser_ref,
    greater_ref,
    coulomb_ref,
    forward_hbm,
    inverse_hbm,
    pattern_ref,
    *refs,
):
    sides = 1 if sections == 2 else 2
    polar_ref = refs[0]
    beside_refs = refs[1 : 1 + sides]
    sum_hbm, right_ref, picked_last_ref, mask_last_ref = refs[1 + sides : 5 + sides]
    (
        forward_ref,
        inverse_ref,
        table_sem,
        other_ref,
        coulomb_near,
        sum_ref,
        picked_ref,
        mask_ref,
        rows_ref,
        sum_sem,
        near_sem,
        x_ref,
        below_ref,
        down_ref,
        partial_ref,
        d_ref,
        in_send,
        in_recv,
        pass_send,
        pass_recv,
        up_send,
        up_recv,
        down_send,
        down_recv,
        out_send,
        out_recv,
        side_send,
        side_recv,
        c_send,
        c_recv,
    ) = refs[5 + sides :]
    tiles = x_ref.shape[1]
    local = polar_ref.shape[0]
    slots = tiles // GROUPS
    some = local // BATCHES
    group = owners // 4
    half = owners // 2
    me = lax.axis_index("el")
    section = lax.axis_index("sec")
    quarter = me // group
    place = lax.rem(me, group)
    base = quarter * group
    half_base = (quarter // 2) * half
    spot = lax.rem(me, half)
    outer = jnp.logical_or(quarter == 0, quarter == 3)
    inward = jnp.where(quarter == 0, me + group, me - group)
    mesh_id = pl.DeviceIdType.MESH
    if sections == 2:
        targets = [1 - section]
    else:
        targets = [
            lax.rem(section + 1, sections),
            lax.rem(section + sections - 1, sections),
        ]

    load_f = pltpu.make_async_copy(forward_hbm, forward_ref, table_sem.at[0])
    load_i = pltpu.make_async_copy(inverse_hbm, inverse_ref, table_sem.at[1])
    load_f.start()
    load_i.start()
    barrier = pltpu.get_barrier_semaphore()

    def greet(step, carry):
        peer = half_base + lax.rem(spot + step, half)
        pl.semaphore_signal(barrier, inc=1, device_id={"el": peer}, device_id_type=mesh_id)
        return carry

    lax.fori_loop(1, half, greet, 0)
    for target in targets:
        pl.semaphore_signal(barrier, inc=1, device_id={"sec": target}, device_id_type=mesh_id)

    @pl.when(quarter < 2)
    def _():
        for peer in range(group):
            pl.semaphore_signal(
                barrier, inc=1, device_id={"el": half + peer}, device_id_type=mesh_id
            )

    @pl.when(quarter == 2)
    def _():
        pl.semaphore_signal(barrier, inc=1, device_id={"el": me - group}, device_id_type=mesh_id)

    greeted = jnp.where(quarter == 2, half, jnp.where(quarter == 1, 1, 0))
    pl.semaphore_wait(barrier, half - 1 + sides + greeted)

    mine = pl.ds(spot * local, local)
    own = pl.ds(lax.rem(quarter, 2) * group * local, group * local)
    theirs = pl.ds((1 - lax.rem(quarter, 2)) * group * local, group * local)

    def send_in(which, source, tile):
        pltpu.make_async_copy(
            source.at[:, place, tile], x_ref.at[which, tile, mine], in_recv.at[which, tile]
        ).start()

        def send(turn, carry):
            peer = lax.rem(place + 1 + turn, group)
            pltpu.make_async_remote_copy(
                src_ref=source.at[:, peer, tile],
                dst_ref=x_ref.at[which, tile, mine],
                send_sem=in_send,
                recv_sem=in_recv.at[which, tile],
                device_id={"el": base + peer},
                device_id_type=mesh_id,
            ).start()
            return carry

        for turn in range(group - 1):
            send(turn, 0)

    def send_both(tile, carry):
        send_in(1, greater_ref, tile)
        send_in(0, lesser_ref, tile)
        return carry

    lax.fori_loop(0, tiles, send_both, 0)

    shared = pltpu.make_async_remote_copy(
        src_ref=coulomb_ref.at[1],
        dst_ref=other_ref,
        send_sem=c_send,
        recv_sem=c_recv,
        device_id={"sec": targets[0]},
        device_id_type=mesh_id,
    )
    shared.start()

    def gathered(which, tile):
        part = x_ref.at[which, tile, own]
        pltpu.make_async_copy(part, part, in_recv.at[which, tile]).wait()

    def pass_inward(which, tile, peer):
        gathered(which, tile)
        pltpu.make_async_remote_copy(
            src_ref=x_ref.at[which, tile, own],
            dst_ref=x_ref.at[which, tile, own],
            send_sem=pass_send,
            recv_sem=pass_recv.at[which, tile],
            device_id={"el": peer},
            device_id_type=mesh_id,
        ).start()

    def passed(which, tile):
        part = x_ref.at[which, tile, theirs]
        pltpu.make_async_copy(part, part, pass_recv.at[which, tile]).wait()

    def forward_copy(tile, side):
        return pltpu.make_async_remote_copy(
            src_ref=polar_ref.at[:, :, tile],
            dst_ref=beside_refs[side].at[:, :, tile],
            send_sem=side_send.at[side, tile],
            recv_sem=side_recv.at[side, tile],
            device_id={"sec": targets[side]},
            device_id_type=mesh_id,
        )

    def pass_on(tile):
        whole = polar_ref.at[:, :, tile]
        pltpu.make_async_copy(whole, whole, out_recv.at[tile]).wait()

        @pl.when(quarter < 2)
        def _():
            part = partial_ref.at[:, :, tile]
            pltpu.make_async_copy(part, part, down_recv.at[tile]).wait()
            both = polar_ref[:, :, tile].astype(jnp.float32)
            both = both + partial_ref[:, :, tile].astype(jnp.float32)
            polar_ref[:, :, tile] = both.astype(jnp.bfloat16)

        for side in range(sides):
            forward_copy(tile, side).start()

    def give(tile):
        pltpu.make_async_copy(
            d_ref.at[tile, mine], polar_ref.at[:, place, tile], out_recv.at[tile]
        ).start()

        def send(turn, carry):
            peer = lax.rem(spot + 1 + turn, half)
            pltpu.make_async_remote_copy(
                src_ref=d_ref.at[tile, pl.ds(peer * local, local)],
                dst_ref=polar_ref.at[:, place, tile],
                send_sem=out_send,
                recv_sem=out_recv.at[tile],
                device_id={"el": half_base + peer},
                device_id_type=mesh_id,
            ).start()
            return carry

        for turn in range(half - 1):
            send(turn, 0)

    def lift(tile):
        gathered(1, tile)
        passed(1, tile)
        pltpu.make_async_remote_copy(
            src_ref=x_ref.at[1, tile],
            dst_ref=below_ref.at[tile],
            send_sem=up_send,
            recv_sem=up_recv.at[tile],
            device_id={"el": me + group},
            device_id_type=mesh_id,
        ).start()
        gathered(0, tile)
        passed(0, tile)
        value = low_part(factor, x_ref[0, tile], x_ref[1, tile], forward_ref, inverse_ref)
        d_ref[tile] = value.astype(jnp.bfloat16).reshape(d_ref.shape[1:])
        give(tile)

    def upper(tile):
        gathered(0, tile)
        gathered(1, tile)
        passed(0, tile)
        passed(1, tile)
        part = below_ref.at[tile]
        pltpu.make_async_copy(part, part, up_recv.at[tile]).wait()
        down, above = high_parts(
            factor, x_ref[0, tile], below_ref[tile], x_ref[1, tile], forward_ref, inverse_ref
        )
        shape = d_ref.shape[1:]
        down_ref[tile] = down.astype(jnp.bfloat16).reshape(shape)
        for peer in range(half):
            pltpu.make_async_remote_copy(
                src_ref=down_ref.at[tile, peer * local : (peer + 1) * local],
                dst_ref=partial_ref.at[:, place, tile],
                send_sem=down_send,
                recv_sem=down_recv.at[tile],
                device_id={"el": peer},
                device_id_type=mesh_id,
            ).start()
        d_ref[tile] = above.astype(jnp.bfloat16).reshape(shape)
        give(tile)

    def prepare():
        pltpu.make_async_copy(coulomb_ref, coulomb_near, near_sem).wait()
        shared.wait_recv()
        screen_setup(
            sections,
            coulomb_near,
            other_ref,
            pattern_ref,
            right_ref,
            picked_ref,
            mask_ref,
            tiles,
        )
        picked_last_ref[...] = picked_ref[GROUPS - 1]
        mask_last_ref[...] = mask_ref[GROUPS - 1]
        for b in range(local):
            sum_ref[b] = jnp.zeros(sum_ref.shape[1:], sum_ref.dtype)

    def sum_copy(batch):
        part = pl.ds(batch * some, some)
        return pltpu.make_async_copy(sum_ref.at[part], sum_hbm.at[part], sum_sem.at[batch])

    def screen_some(turn):
        chunk = turn // BATCHES
        batch = lax.rem(turn, BATCHES)

        @pl.when(batch == 0)
        def _():
            for s in range(slots):
                for side in range(sides):
                    forward_copy(chunk * slots + s, side).wait_recv()

        start = batch * some
        columns = pl.ds(chunk * slots, slots)
        sources = [polar_ref, *beside_refs]
        for t in range(1 + sides):
            for b in range(some):
                piece = sources[t][start + b, :, columns]
                rows_ref[t, b] = piece.reshape(rows_ref.shape[2:]).astype(jnp.float32)
        masks = [mask_ref[chunk, t] for t in range(1 + sides)]
        added = screen_chunk(some, rows_ref, masks, right_ref, picked_ref[chunk])
        for b in range(some):
            for c in range(2):
                old = sum_ref[start + b, c].astype(jnp.float32)
                sum_ref[start + b, c] = (old + added[2 * b + c]).astype(jnp.bfloat16)

        @pl.when(chunk == GROUPS - 2)
        def _():
            sum_copy(batch).start()

    pltpu.make_async_copy(coulomb_ref, coulomb_near, near_sem).start()
    load_f.wait()
    load_i.wait()
    turns = (GROUPS - 1) * BATCHES
    lead = slots + 2
    stride = max(1, slots // BATCHES)
    last = max(tiles, (turns - 1) * stride + 1 + lead)
    behind = 6
    delay = jnp.where(outer, tiles, jnp.where(quarter == 1, behind, 2))
    ready = jnp.where(outer, tiles, jnp.where(quarter == 1, 3, 0))

    def body(i, carry):
        @pl.when(jnp.logical_and(outer, i < tiles))
        def _():
            pass_inward(1, i, inward)
            pass_inward(0, i, inward)

        @pl.when(jnp.logical_and(quarter == 1, i < tiles))
        def _():
            lift(i)

        @pl.when(i == ready)
        def _():
            prepare()

        @pl.when(jnp.logical_and(quarter == 2, i < tiles))
        def _():
            upper(i)

        tile = i - delay

        @pl.when(jnp.logical_and(tile >= 0, tile < tiles))
        def _():
            pass_on(tile)

        since = tile - lead
        turn = since // stride

        @pl.when(
            jnp.logical_and(since >= 0, jnp.logical_and(since % stride == 0, turn < turns))
        )
        def _():
            screen_some(turn)

        return carry

    lax.fori_loop(0, last + delay, body, 0)

    @pl.when(outer)
    def _():
        part = x_ref.at[:, :, own]
        pltpu.make_async_copy(part, part, pass_send).wait()

    @pl.when(jnp.logical_not(outer))
    def _():
        part = d_ref.at[:, pl.ds(0, (half - 1) * local)]
        pltpu.make_async_copy(part, part, out_send).wait()

    @pl.when(quarter == 1)
    def _():
        pltpu.make_async_copy(below_ref, below_ref, up_send).wait()

    @pl.when(quarter == 2)
    def _():
        pltpu.make_async_copy(down_ref, down_ref, down_send).wait()

    part = x_ref.at[:, :, pl.ds(0, (group - 1) * local)]
    pltpu.make_async_copy(part, part, in_send).wait()
    for batch in range(BATCHES):
        sum_copy(batch).wait()

    def settle_sent(tile, carry):
        for side in range(sides):
            forward_copy(tile, side).wait_send()
        return carry

    def settle(tile, carry):
        for side in range(sides):
            forward_copy(tile, side).wait()
        return carry

    lax.fori_loop(0, (GROUPS - 1) * slots, settle_sent, 0)
    lax.fori_loop((GROUPS - 1) * slots, tiles, settle, 0)
    shared.wait_send()


def exchange(owners, sections, lesser, greater, coulomb, pattern):
    local, count, _, width = lesser.shape
    group = owners // 4
    tiles = count // group
    energies = local * owners
    depth = energies // 2
    nb = coulomb.shape[1]
    sides = 1 if sections == 2 else 2
    terms = 1 + sides
    chunk = count // GROUPS
    forward, inverse = tables(energies)
    split = (local, group, tiles, 2, width)
    bf16 = jnp.bfloat16
    tile_shape = jax.ShapeDtypeStruct(split, bf16)
    anywhere = pl.BlockSpec(memory_space=pl.ANY)
    near = pl.BlockSpec(memory_space=pltpu.VMEM)
    dma = pltpu.SemaphoreType.DMA
    buffer = pltpu.VMEM((tiles, depth, 2, width), bf16)
    return pl.pallas_call(
        functools.partial(exchange_kernel, owners, sections, 1.0 / (energies * energies**0.5)),
        in_specs=[anywhere] * 5 + [near],
        out_specs=[near] * (1 + sides) + [anywhere] + [near] * 3,
        out_shape=[tile_shape] * (1 + sides)
        + [
            jax.ShapeDtypeStruct((local, 2, nb, nb), bf16),
            jax.ShapeDtypeStruct((terms, nb, nb), bf16),
            jax.ShapeDtypeStruct((nb, terms * TR * chunk), bf16),
            jax.ShapeDtypeStruct((terms, chunk, nb), bf16),
        ],
        scratch_shapes=[
            pltpu.VMEM(forward.shape, bf16),
            pltpu.VMEM(inverse.shape, bf16),
            dma((2,)),
            pltpu.VMEM((nb, nb), bf16),
            pltpu.VMEM(coulomb.shape, bf16),
            pltpu.VMEM((local, 2, nb, nb), bf16),
            pltpu.VMEM((GROUPS, nb, terms * TR * chunk), bf16),
            pltpu.VMEM((GROUPS, terms, chunk, nb), bf16),
            pltpu.VMEM((terms, local // BATCHES, 2 * chunk, width), jnp.float32),
            dma((BATCHES,)),
            dma(()),
            pltpu.VMEM((2, tiles, depth, 2, width), bf16),
            buffer,
            buffer,
            pltpu.VMEM(split, bf16),
            buffer,
            dma(()),
            dma((2, tiles)),
            dma(()),
            dma((2, tiles)),
            dma(()),
            dma((tiles,)),
            dma(()),
            dma((tiles,)),
            dma(()),
            dma((tiles,)),
            dma((sides, tiles)),
            dma((sides, tiles)),
            dma(()),
            dma(()),
        ],
        compiler_params=pltpu.CompilerParams(
            collective_id=0, has_side_effects=True, vmem_limit_bytes=VMEM_LIMIT
        ),
    )(lesser.reshape(split), greater.reshape(split), coulomb, forward, inverse, pattern)


def screen_setup(
    sections, coulomb_ref, other_ref, pattern_ref, right_ref, picked_ref, mask_ref, tiles
):
    groups, terms, chunk, nb = mask_ref.shape
    count = groups * chunk
    slots = tiles // groups
    section = lax.axis_index("sec")
    lower = other_ref[...].astype(jnp.float32).T
    upper = coulomb_ref[1].astype(jnp.float32)
    matrices = [coulomb_ref[0].astype(jnp.float32)]
    if sections == 2:
        sources = [section, 1 - section]
        matrices.append(jnp.where(section == 0, upper, lower))
    else:
        sources = [
            section,
            lax.rem(section + sections - 1, sections),
            lax.rem(section + 1, sections),
        ]
        matrices.append(jnp.where(section > 0, lower, 0.0))
        matrices.append(jnp.where(section < sections - 1, upper, 0.0))
    across = nb // TC
    wide = TR * count
    iota = lambda shape, axis: lax.broadcasted_iota(jnp.int32, shape, axis)
    row_of = iota((nb, wide), 0)
    lane = iota((count, wide), 1)
    member = lane % chunk
    listed_at = (member // slots) * tiles + lane // (TR * chunk) * slots + member % slots
    taken = listed_at == iota((count, wide), 0)
    inner_row = iota((1, wide), 1) // chunk % TR
    diagonal = iota((count, count), 0) == iota((count, count), 1)
    member = iota((chunk, count), 0)
    begin = (member // slots) * tiles + member % slots
    column_of = iota((chunk, nb), 1) // TC
    for t in range(terms):
        listed = pattern_ref[pl.ds(sources[t], 1), :].astype(jnp.float32)
        upright = jnp.sum(jnp.where(diagonal, listed, 0.0), axis=1, keepdims=True)
        spread = jnp.sum(jnp.where(taken, upright, 0.0), axis=0, keepdims=True).astype(jnp.int32)
        row = spread // across * TR + inner_row
        chosen = jnp.where(row_of == row, 1.0, 0.0).astype(jnp.bfloat16)
        picked = dot32(matrices[t].astype(jnp.bfloat16), chosen).astype(jnp.bfloat16)
        span = TR * chunk
        for g in range(groups):
            picked_ref[g, :, t * span : (t + 1) * span] = picked[:, g * span : (g + 1) * span]
            here = iota((chunk, count), 1) == begin + g * slots
            place = jnp.sum(jnp.where(here, listed, 0.0), axis=1, keepdims=True).astype(jnp.int32)
            mask_ref[g, t] = jnp.where(column_of == place % across, 1.0, 0.0).astype(jnp.bfloat16)
        right_ref[t] = matrices[t].T.astype(jnp.bfloat16)


def screen_chunk(batch, rows_ref, masks, right_ref, picked):
    terms = len(masks)
    chunk, nb = masks[0].shape
    width = rows_ref.shape[-1]
    lane = lax.broadcasted_iota(jnp.int32, (chunk, width), 1) % TC
    halves = []
    for t in range(terms):
        stacked = []
        for b in range(batch):
            for c in range(2):
                tile = rows_ref[t, b, pl.ds(c, chunk, stride=2), :]
                for r in range(TR):
                    spread = jnp.take_along_axis(
                        tile, lane + r * TC, axis=1, mode="promise_in_bounds"
                    ).astype(jnp.bfloat16)
                    stacked.append(jnp.concatenate([spread] * (nb // width), axis=1) * masks[t])
        stacked = jnp.concatenate(stacked, axis=0)
        halves.append(dot32(stacked, right_ref[t]).astype(jnp.bfloat16))
    span = TR * chunk
    added = []
    for n in range(2 * batch):
        part = jnp.concatenate([h[n * span : (n + 1) * span] for h in halves], axis=0)
        added.append(dot32(picked, part))
    return added


def screen_kernel(terms, batch, *refs):
    tile_refs = refs[:terms]
    polar_ref, sum_ref, right_ref, picked_ref, mask_ref = refs[terms : terms + 5]
    polar_out, out_ref, rows_ref = refs[terms + 5 :]
    polar_out[...] = polar_ref[...]
    for t in range(terms):
        for b in range(batch):
            rows_ref[t, b] = tile_refs[t][b].reshape(rows_ref.shape[2:]).astype(jnp.float32)
    masks = [mask_ref[t] for t in range(terms)]
    added = screen_chunk(batch, rows_ref, masks, right_ref, picked_ref[...])
    for b in range(batch):
        for c in range(2):
            out_ref[b, c] = (sum_ref[b, c].astype(jnp.float32) + added[2 * b + c]).astype(
                jnp.bfloat16
            )


def screen(tiles, total, right, picked, mask):
    terms = len(tiles)
    local, group, per, _, width = tiles[0].shape
    chunk, nb = mask.shape[1:]
    batch = local // BATCHES
    slots = per // GROUPS
    whole = lambda array: pl.BlockSpec(array.shape, lambda i: (0,) * array.ndim)
    some = pl.BlockSpec((batch, group, slots, 2, width), lambda i: (i, 0, GROUPS - 1, 0, 0))
    full = pl.BlockSpec((batch, group, per, 2, width), lambda i: (i, 0, 0, 0, 0))
    square = pl.BlockSpec((batch, 2, nb, nb), lambda i: (i, 0, 0, 0))
    return pl.pallas_call(
        functools.partial(screen_kernel, terms, batch),
        grid=(BATCHES,),
        in_specs=[some] * terms + [full, square, whole(right), whole(picked), whole(mask)],
        out_specs=[full, square],
        out_shape=[
            jax.ShapeDtypeStruct(tiles[0].shape, jnp.bfloat16),
            jax.ShapeDtypeStruct(total.shape, jnp.bfloat16),
        ],
        scratch_shapes=[pltpu.VMEM((terms, batch, 2 * chunk, width), jnp.float32)],
        compiler_params=pltpu.CompilerParams(vmem_limit_bytes=VMEM_LIMIT),
    )(*tiles, tiles[0], total, right, picked, mask)


def on_device(sections, owners, green_lesser, green_greater, coulomb, pattern):
    _, local, count, _, width = green_lesser.shape
    sides = 1 if sections == 2 else 2
    results = exchange(
        owners, sections, green_lesser[0], green_greater[0], coulomb[0], pattern
    )
    polar, screened = screen(results[: 1 + sides], *results[1 + sides :])
    return polar.reshape(1, local, count, 2, width), screened[None]


def solution(mesh):
    in_specs = (
        P("sec", "el", None, None, None),
        P("sec", "el", None, None, None),
        P("sec", None, None, None),
        P(),
    )
    out_specs = (P("sec", "el", None, None, None), P("sec", "el", None, None, None))
    return jax.shard_map(
        functools.partial(on_device, mesh.shape["sec"], mesh.shape["el"]),
        mesh=mesh,
        in_specs=in_specs,
        out_specs=out_specs,
        check_vma=False,
    )
```

```python
import functools

import jax
import jax.numpy as jnp
import numpy as np
from jax import lax
from jax.experimental import pallas as pl
from jax.experimental.pallas import tpu as pltpu
from jax.sharding import PartitionSpec as P

TR = 8
TC = 16
VMEM_LIMIT = 40 * 1024 * 1024
GROUPS = 4
BATCHES = 2
STEPS = 4


def tables(energies):
    length = energies
    depth = energies // 2
    order = np.concatenate([np.arange(0, length, 2), np.arange(1, length, 2)])
    phase = np.outer(order, np.arange(depth)) % length
    phase = phase * (2.0 * np.pi / length)
    cosine = np.cos(phase).astype(np.float32)
    sine = np.sin(phase).astype(np.float32)
    real = np.stack([cosine, sine], axis=2).reshape(length, length)
    imag = np.stack([-sine, cosine], axis=2).reshape(length, length)
    forward = np.concatenate([real, imag], axis=0)
    out_r = np.concatenate([-sine.T, -cosine.T], axis=1)
    out_i = np.concatenate([cosine.T, -sine.T], axis=1)
    inverse = np.stack([out_r, out_i], axis=1).reshape(length, 2 * length)
    return jnp.asarray(forward, jnp.bfloat16), jnp.asarray(inverse, jnp.bfloat16)


def dot32(a, b):
    return jnp.dot(a, b, preferred_element_type=jnp.float32)


def conjugate_product(a, b):
    (ar, ai), (br, bi) = a, b
    return jnp.concatenate([ar * br + ai * bi, ai * br - ar * bi], axis=0).astype(jnp.bfloat16)


def spectra(parts, forward_ref):
    depth, _, width = parts[0].shape
    length = 2 * depth
    joined = jnp.concatenate([p.reshape(length, width) for p in parts], axis=1)
    z = dot32(forward_ref[...], joined)
    return [
        (z[:length, i * width : (i + 1) * width], z[length:, i * width : (i + 1) * width])
        for i in range(len(parts))
    ]


def low_part(factor, lesser, greater, forward_ref, inverse_ref):
    first, second = spectra([lesser, greater], forward_ref)
    return dot32(inverse_ref[...], conjugate_product(first, second)) * factor


def high_parts(factor, lesser, below, greater, forward_ref, inverse_ref):
    width = lesser.shape[-1]
    first, under, second = spectra([lesser, below, greater], forward_ref)
    middle = under[0].shape[0] // 2

    def shifted(a, b):
        return jnp.concatenate([b[:middle] + a[:middle], b[middle:] - a[middle:]], axis=0)

    both = tuple(shifted(a, b) for a, b in zip(under, second))
    product = jnp.concatenate(
        [conjugate_product(first, both), conjugate_product(first, under)], axis=1
    )
    series = dot32(inverse_ref[...], product) * factor
    return series[:, :width], series[:, width:]


def exchange_kernel(
    owners,
    sections,
    factor,
    lesser_ref,
    greater_ref,
    coulomb_ref,
    forward_hbm,
    inverse_hbm,
    pattern_hbm,
    *refs,
):
    sides = 1 if sections == 2 else 2
    polar_ref = refs[0]
    beside_refs = refs[1 : 1 + sides]
    sum_ref, right_ref, picked_last_ref, mask_last_ref = refs[1 + sides : 5 + sides]
    (
        pattern_ref,
        forward_ref,
        inverse_ref,
        table_sem,
        other_ref,
        coulomb_near,
        picked_ref,
        mask_ref,
        rows_ref,
        near_sem,
        x_ref,
        below_ref,
        down_ref,
        partial_ref,
        d_ref,
        in_send,
        in_recv,
        pass_send,
        pass_recv,
        up_send,
        up_recv,
        down_send,
        down_recv,
        out_send,
        out_recv,
        side_send,
        side_recv,
        c_send,
        c_recv,
    ) = refs[5 + sides :]
    tiles = x_ref.shape[1]
    local = polar_ref.shape[0]
    slots = tiles // GROUPS
    some = local // BATCHES
    group = owners // 4
    half = owners // 2
    me = lax.axis_index("el")
    section = lax.axis_index("sec")
    quarter = me // group
    place = lax.rem(me, group)
    base = quarter * group
    half_base = (quarter // 2) * half
    spot = lax.rem(me, half)
    outer = jnp.logical_or(quarter == 0, quarter == 3)
    inward = jnp.where(quarter == 0, me + group, me - group)
    mesh_id = pl.DeviceIdType.MESH
    if sections == 2:
        targets = [1 - section]
    else:
        targets = [
            lax.rem(section + 1, sections),
            lax.rem(section + sections - 1, sections),
        ]

    load_f = pltpu.make_async_copy(forward_hbm, forward_ref, table_sem.at[0])
    load_i = pltpu.make_async_copy(inverse_hbm, inverse_ref, table_sem.at[1])
    load_p = pltpu.make_async_copy(pattern_hbm, pattern_ref, table_sem.at[2])
    load_f.start()
    load_i.start()
    load_p.start()
    barrier = pltpu.get_barrier_semaphore()

    def greet(step, carry):
        peer = half_base + lax.rem(spot + step, half)
        pl.semaphore_signal(barrier, inc=1, device_id={"el": peer}, device_id_type=mesh_id)
        return carry

    lax.fori_loop(1, half, greet, 0)
    for target in targets:
        pl.semaphore_signal(barrier, inc=1, device_id={"sec": target}, device_id_type=mesh_id)

    @pl.when(quarter < 2)
    def _():
        for peer in range(group):
            pl.semaphore_signal(
                barrier, inc=1, device_id={"el": half + peer}, device_id_type=mesh_id
            )

    @pl.when(quarter == 2)
    def _():
        pl.semaphore_signal(barrier, inc=1, device_id={"el": me - group}, device_id_type=mesh_id)

    greeted = jnp.where(quarter == 2, half, jnp.where(quarter == 1, 1, 0))
    pl.semaphore_wait(barrier, half - 1 + sides + greeted)

    mine = pl.ds(spot * local, local)
    own = pl.ds(lax.rem(quarter, 2) * group * local, group * local)
    theirs = pl.ds((1 - lax.rem(quarter, 2)) * group * local, group * local)

    def send_in(which, source, tile):
        pltpu.make_async_copy(
            source.at[:, place, tile], x_ref.at[which, tile, mine], in_recv.at[which, tile]
        ).start()

        def send(turn, carry):
            peer = lax.rem(place + 1 + turn, group)
            pltpu.make_async_remote_copy(
                src_ref=source.at[:, peer, tile],
                dst_ref=x_ref.at[which, tile, mine],
                send_sem=in_send,
                recv_sem=in_recv.at[which, tile],
                device_id={"el": base + peer},
                device_id_type=mesh_id,
            ).start()
            return carry

        for turn in range(group - 1):
            send(turn, 0)

    def send_both(tile, carry):
        send_in(1, greater_ref, tile)
        send_in(0, lesser_ref, tile)
        return carry

    lax.fori_loop(0, tiles, send_both, 0)

    shared = pltpu.make_async_remote_copy(
        src_ref=coulomb_ref.at[1],
        dst_ref=other_ref,
        send_sem=c_send,
        recv_sem=c_recv,
        device_id={"sec": targets[0]},
        device_id_type=mesh_id,
    )
    shared.start()

    def gathered(which, tile):
        part = x_ref.at[which, tile, own]
        pltpu.make_async_copy(part, part, in_recv.at[which, tile]).wait()

    def pass_inward(which, tile, peer):
        gathered(which, tile)
        pltpu.make_async_remote_copy(
            src_ref=x_ref.at[which, tile, own],
            dst_ref=x_ref.at[which, tile, own],
            send_sem=pass_send,
            recv_sem=pass_recv.at[which, tile],
            device_id={"el": peer},
            device_id_type=mesh_id,
        ).start()

    def passed(which, tile):
        part = x_ref.at[which, tile, theirs]
        pltpu.make_async_copy(part, part, pass_recv.at[which, tile]).wait()

    def forward_copy(tile, side):
        return pltpu.make_async_remote_copy(
            src_ref=polar_ref.at[:, :, tile],
            dst_ref=beside_refs[side].at[:, :, tile],
            send_sem=side_send.at[side, tile],
            recv_sem=side_recv.at[side, tile],
            device_id={"sec": targets[side]},
            device_id_type=mesh_id,
        )

    def pass_on(tile):
        whole = polar_ref.at[:, :, tile]
        pltpu.make_async_copy(whole, whole, out_recv.at[tile]).wait()

        @pl.when(quarter < 2)
        def _():
            part = partial_ref.at[:, :, tile]
            pltpu.make_async_copy(part, part, down_recv.at[tile]).wait()
            both = polar_ref[:, :, tile].astype(jnp.float32)
            both = both + partial_ref[:, :, tile].astype(jnp.float32)
            polar_ref[:, :, tile] = both.astype(jnp.bfloat16)

        for side in range(sides):
            forward_copy(tile, side).start()

    def give(tile):
        pltpu.make_async_copy(
            d_ref.at[tile, mine], polar_ref.at[:, place, tile], out_recv.at[tile]
        ).start()

        def send(turn, carry):
            peer = lax.rem(spot + 1 + turn, half)
            pltpu.make_async_remote_copy(
                src_ref=d_ref.at[tile, pl.ds(peer * local, local)],
                dst_ref=polar_ref.at[:, place, tile],
                send_sem=out_send,
                recv_sem=out_recv.at[tile],
                device_id={"el": half_base + peer},
                device_id_type=mesh_id,
            ).start()
            return carry

        for turn in range(half - 1):
            send(turn, 0)

    def lift(tile):
        gathered(1, tile)
        passed(1, tile)
        pltpu.make_async_remote_copy(
            src_ref=x_ref.at[1, tile],
            dst_ref=below_ref.at[tile],
            send_sem=up_send,
            recv_sem=up_recv.at[tile],
            device_id={"el": me + group},
            device_id_type=mesh_id,
        ).start()
        gathered(0, tile)
        passed(0, tile)
        value = low_part(factor, x_ref[0, tile], x_ref[1, tile], forward_ref, inverse_ref)
        d_ref[tile] = value.astype(jnp.bfloat16).reshape(d_ref.shape[1:])
        give(tile)

    def upper(tile):
        gathered(0, tile)
        gathered(1, tile)
        passed(0, tile)
        passed(1, tile)
        part = below_ref.at[tile]
        pltpu.make_async_copy(part, part, up_recv.at[tile]).wait()
        down, above = high_parts(
            factor, x_ref[0, tile], below_ref[tile], x_ref[1, tile], forward_ref, inverse_ref
        )
        shape = d_ref.shape[1:]
        down_ref[tile] = down.astype(jnp.bfloat16).reshape(shape)
        for peer in range(half):
            pltpu.make_async_remote_copy(
                src_ref=down_ref.at[tile, peer * local : (peer + 1) * local],
                dst_ref=partial_ref.at[:, place, tile],
                send_sem=down_send,
                recv_sem=down_recv.at[tile],
                device_id={"el": peer},
                device_id_type=mesh_id,
            ).start()
        d_ref[tile] = above.astype(jnp.bfloat16).reshape(shape)
        give(tile)

    def prepare():
        pltpu.make_async_copy(coulomb_ref, coulomb_near, near_sem).wait()
        shared.wait_recv()
        screen_setup(
            sections,
            coulomb_near,
            other_ref,
            pattern_ref,
            right_ref,
            picked_ref,
            mask_ref,
            tiles,
        )
        picked_last_ref[...] = picked_ref[GROUPS - 1]
        mask_last_ref[...] = mask_ref[GROUPS - 1]
        for b in range(local):
            sum_ref[b] = jnp.zeros(sum_ref.shape[1:], sum_ref.dtype)

    def screen_some(turn):
        chunk = turn // BATCHES
        batch = lax.rem(turn, BATCHES)

        @pl.when(batch == 0)
        def _():
            for s in range(slots):
                for side in range(sides):
                    forward_copy(chunk * slots + s, side).wait_recv()

        start = batch * some
        columns = pl.ds(chunk * slots, slots)
        sources = [polar_ref, *beside_refs]
        for t in range(1 + sides):
            for b in range(some):
                piece = sources[t][start + b, :, columns]
                rows_ref[t, b] = piece.reshape(rows_ref.shape[2:]).astype(jnp.float32)
        masks = [mask_ref[chunk, t] for t in range(1 + sides)]
        added = screen_chunk(some, rows_ref, masks, right_ref, picked_ref[chunk])
        for b in range(some):
            for c in range(2):
                old = sum_ref[start + b, c].astype(jnp.float32)
                sum_ref[start + b, c] = (old + added[2 * b + c]).astype(jnp.bfloat16)

    pltpu.make_async_copy(coulomb_ref, coulomb_near, near_sem).start()
    load_f.wait()
    load_i.wait()
    load_p.wait()
    turns = (GROUPS - 1) * BATCHES
    lead = slots + 1
    stride = max(1, slots // BATCHES)
    last = max(tiles, (turns - 1) * stride + 1 + lead)
    behind = 6
    delay = jnp.where(outer, tiles, jnp.where(quarter == 1, behind, 3))
    ready = jnp.where(outer, tiles, jnp.where(quarter == 1, 3, 0))

    def body(i, carry):
        @pl.when(jnp.logical_and(outer, i < tiles))
        def _():
            pass_inward(1, i, inward)
            pass_inward(0, i, inward)

        @pl.when(jnp.logical_and(quarter == 1, i < tiles))
        def _():
            lift(i)

        @pl.when(i == ready)
        def _():
            prepare()

        @pl.when(jnp.logical_and(quarter == 2, i < tiles))
        def _():
            upper(i)

        tile = i - delay

        @pl.when(jnp.logical_and(tile >= 0, tile < tiles))
        def _():
            pass_on(tile)

        since = tile - lead
        turn = since // stride

        @pl.when(
            jnp.logical_and(since >= 0, jnp.logical_and(since % stride == 0, turn < turns))
        )
        def _():
            screen_some(turn)

        return carry

    lax.fori_loop(0, last + delay, body, 0)

    @pl.when(outer)
    def _():
        part = x_ref.at[:, :, own]
        pltpu.make_async_copy(part, part, pass_send).wait()

    @pl.when(jnp.logical_not(outer))
    def _():
        part = d_ref.at[:, pl.ds(0, (half - 1) * local)]
        pltpu.make_async_copy(part, part, out_send).wait()

    @pl.when(quarter == 1)
    def _():
        pltpu.make_async_copy(below_ref, below_ref, up_send).wait()

    @pl.when(quarter == 2)
    def _():
        pltpu.make_async_copy(down_ref, down_ref, down_send).wait()

    part = x_ref.at[:, :, pl.ds(0, (group - 1) * local)]
    pltpu.make_async_copy(part, part, in_send).wait()

    def settle_sent(tile, carry):
        for side in range(sides):
            forward_copy(tile, side).wait_send()
        return carry

    def settle(tile, carry):
        for side in range(sides):
            forward_copy(tile, side).wait()
        return carry

    lax.fori_loop(0, (GROUPS - 1) * slots, settle_sent, 0)
    lax.fori_loop((GROUPS - 1) * slots, tiles, settle, 0)
    shared.wait_send()


def exchange(owners, sections, lesser, greater, coulomb, pattern):
    local, count, _, width = lesser.shape
    group = owners // 4
    tiles = count // group
    energies = local * owners
    depth = energies // 2
    nb = coulomb.shape[1]
    sides = 1 if sections == 2 else 2
    terms = 1 + sides
    chunk = count // GROUPS
    forward, inverse = tables(energies)
    split = (local, group, tiles, 2, width)
    bf16 = jnp.bfloat16
    far = pl.BlockSpec(memory_space=pltpu.HBM)
    near = pl.BlockSpec(memory_space=pltpu.VMEM)
    dma = pltpu.SemaphoreType.DMA
    buffer = pltpu.VMEM((tiles, depth, 2, width), bf16)
    operands = [lesser.reshape(split), greater.reshape(split), coulomb, forward, inverse, pattern]
    return pl.pallas_call(
        functools.partial(exchange_kernel, owners, sections, 1.0 / (energies * energies**0.5)),
        in_specs=[far] * 6,
        out_specs=[near] * (5 + sides),
        out_shape=[pltpu.VMEM(split, bf16)] * (1 + sides)
        + [
            pltpu.VMEM((local, 2, nb, nb), bf16),
            pltpu.VMEM((terms, nb, nb), bf16),
            pltpu.VMEM((nb, terms * TR * chunk), bf16),
            pltpu.VMEM((terms, chunk, nb), bf16),
        ],
        scratch_shapes=[
            pltpu.VMEM(pattern.shape, pattern.dtype),
            pltpu.VMEM(forward.shape, bf16),
            pltpu.VMEM(inverse.shape, bf16),
            dma((3,)),
            pltpu.VMEM((nb, nb), bf16),
            pltpu.VMEM(coulomb.shape, bf16),
            pltpu.VMEM((GROUPS, nb, terms * TR * chunk), bf16),
            pltpu.VMEM((GROUPS, terms, chunk, nb), bf16),
            pltpu.VMEM((terms, local // BATCHES, 2 * chunk, width), jnp.float32),
            dma(()),
            pltpu.VMEM((2, tiles, depth, 2, width), bf16),
            buffer,
            buffer,
            pltpu.VMEM(split, bf16),
            buffer,
            dma(()),
            dma((2, tiles)),
            dma(()),
            dma((2, tiles)),
            dma(()),
            dma((tiles,)),
            dma(()),
            dma((tiles,)),
            dma(()),
            dma((tiles,)),
            dma((sides, tiles)),
            dma((sides, tiles)),
            dma(()),
            dma(()),
        ],
        compiler_params=pltpu.CompilerParams(
            collective_id=0, has_side_effects=True, vmem_limit_bytes=VMEM_LIMIT
        ),
    )(*[pltpu.with_memory_space_constraint(array, pltpu.HBM) for array in operands])


def screen_setup(
    sections, coulomb_ref, other_ref, pattern_ref, right_ref, picked_ref, mask_ref, tiles
):
    groups, terms, chunk, nb = mask_ref.shape
    count = groups * chunk
    slots = tiles // groups
    section = lax.axis_index("sec")
    lower = other_ref[...].astype(jnp.float32).T
    upper = coulomb_ref[1].astype(jnp.float32)
    matrices = [coulomb_ref[0].astype(jnp.float32)]
    if sections == 2:
        sources = [section, 1 - section]
        matrices.append(jnp.where(section == 0, upper, lower))
    else:
        sources = [
            section,
            lax.rem(section + sections - 1, sections),
            lax.rem(section + 1, sections),
        ]
        matrices.append(jnp.where(section > 0, lower, 0.0))
        matrices.append(jnp.where(section < sections - 1, upper, 0.0))
    across = nb // TC
    wide = TR * count
    iota = lambda shape, axis: lax.broadcasted_iota(jnp.int32, shape, axis)
    row_of = iota((nb, wide), 0)
    lane = iota((count, wide), 1)
    member = lane % chunk
    listed_at = (member // slots) * tiles + lane // (TR * chunk) * slots + member % slots
    taken = listed_at == iota((count, wide), 0)
    inner_row = iota((1, wide), 1) // chunk % TR
    diagonal = iota((count, count), 0) == iota((count, count), 1)
    member = iota((chunk, count), 0)
    begin = (member // slots) * tiles + member % slots
    column_of = iota((chunk, nb), 1) // TC
    for t in range(terms):
        listed = pattern_ref[pl.ds(sources[t], 1), :].astype(jnp.float32)
        upright = jnp.sum(jnp.where(diagonal, listed, 0.0), axis=1, keepdims=True)
        spread = jnp.sum(jnp.where(taken, upright, 0.0), axis=0, keepdims=True).astype(jnp.int32)
        row = spread // across * TR + inner_row
        chosen = jnp.where(row_of == row, 1.0, 0.0).astype(jnp.bfloat16)
        picked = dot32(matrices[t].astype(jnp.bfloat16), chosen).astype(jnp.bfloat16)
        span = TR * chunk
        for g in range(groups):
            picked_ref[g, :, t * span : (t + 1) * span] = picked[:, g * span : (g + 1) * span]
            here = iota((chunk, count), 1) == begin + g * slots
            place = jnp.sum(jnp.where(here, listed, 0.0), axis=1, keepdims=True).astype(jnp.int32)
            mask_ref[g, t] = jnp.where(column_of == place % across, 1.0, 0.0).astype(jnp.bfloat16)
        right_ref[t] = matrices[t].T.astype(jnp.bfloat16)


def right_part(batch, rows, mask, right):
    chunk, nb = mask.shape
    width = rows.shape[-1]
    lane = lax.broadcasted_iota(jnp.int32, (chunk, width), 1) % TC
    stacked = []
    for b in range(batch):
        for c in range(2):
            tile = rows[b, pl.ds(c, chunk, stride=2), :]
            for r in range(TR):
                spread = jnp.take_along_axis(
                    tile, lane + r * TC, axis=1, mode="promise_in_bounds"
                ).astype(jnp.bfloat16)
                stacked.append(jnp.concatenate([spread] * (nb // width), axis=1) * mask)
    return dot32(jnp.concatenate(stacked, axis=0), right).astype(jnp.bfloat16)


def screen_chunk(batch, rows_ref, masks, right_ref, picked):
    span = TR * masks[0].shape[0]
    halves = [
        right_part(batch, rows_ref.at[t], mask, right_ref[t]) for t, mask in enumerate(masks)
    ]
    added = []
    for n in range(2 * batch):
        part = jnp.concatenate([h[n * span : (n + 1) * span] for h in halves], axis=0)
        added.append(dot32(picked, part))
    return added


def screen_kernel(terms, batch, *refs):
    tile_refs = refs[:terms]
    sum_ref, right_ref, picked_ref, mask_ref, polar_out, out_hbm = refs[terms : terms + 6]
    total_ref, rows_ref, half_ref, keep_sem, total_sem = refs[terms + 6 :]
    polar_ref = tile_refs[0]
    local, _, per, _, _ = polar_ref.shape
    slots = per // GROUPS
    steps = local // batch
    def store(step):
        part = pl.ds(step * batch, batch)
        return pltpu.make_async_copy(total_ref.at[part], out_hbm.at[part], total_sem.at[step])

    keep = pltpu.make_async_copy(polar_ref, polar_out, keep_sem)
    keep.start()
    masks = [mask_ref[t] for t in range(terms)]

    span = TR * mask_ref.shape[1]
    wide = local // max(1, local // 16)

    def fill(step, carry):
        for t in range(terms):
            for b in range(wide):
                e = step * wide + b
                piece = tile_refs[t][e, :, per - slots :]
                rows_ref[t, b] = piece.reshape(rows_ref.shape[2:]).astype(jnp.float32)
            half = right_part(wide, rows_ref.at[t], masks[t], right_ref[t])
            half_ref[pl.ds(step * wide * 2, wide * 2), t * span : (t + 1) * span] = half.reshape(
                wide * 2, span, half.shape[-1]
            )
        return carry

    lax.fori_loop(0, local // wide, fill, 0)

    def body(step, carry):
        for b in range(batch):
            for c in range(2):
                e = step * batch + b
                total = dot32(picked_ref[...], half_ref[2 * e + c])
                total = total + sum_ref[e, c].astype(jnp.float32)
                total_ref[e, c] = total.astype(jnp.bfloat16)
        store(step).start()
        return carry

    for step in range(steps):
        body(step, 0)
    keep.wait()
    for step in range(steps):
        store(step).wait()


def screen(tiles, total, right, picked, mask):
    terms = len(tiles)
    local, _, _, _, width = tiles[0].shape
    chunk = mask.shape[1]
    batch = max(1, local // STEPS)
    dma = pltpu.SemaphoreType.DMA
    return pl.pallas_call(
        functools.partial(screen_kernel, terms, batch),
        in_specs=[pl.BlockSpec(memory_space=pltpu.VMEM)] * (terms + 4),
        out_specs=[pl.BlockSpec(memory_space=pltpu.HBM)] * 2,
        out_shape=[
            jax.ShapeDtypeStruct(tiles[0].shape, jnp.bfloat16),
            jax.ShapeDtypeStruct(total.shape, total.dtype),
        ],
        scratch_shapes=[
            pltpu.VMEM(total.shape, total.dtype),
            pltpu.VMEM((terms, local, 2 * chunk, width), jnp.float32),
            pltpu.VMEM((2 * local, terms * TR * chunk, total.shape[-1]), jnp.bfloat16),
            dma(()),
            dma((local // batch,)),
        ],
        compiler_params=pltpu.CompilerParams(vmem_limit_bytes=VMEM_LIMIT),
    )(*tiles, total, right, picked, mask)


def on_device(sections, owners, green_lesser, green_greater, coulomb, pattern):
    _, local, count, _, width = green_lesser.shape
    sides = 1 if sections == 2 else 2
    results = exchange(
        owners, sections, green_lesser[0], green_greater[0], coulomb[0], pattern
    )
    polar, screened = screen(results[: 1 + sides], *results[1 + sides :])
    return polar.reshape(1, local, count, 2, width), screened[None]


def solution(mesh):
    in_specs = (
        P("sec", "el", None, None, None),
        P("sec", "el", None, None, None),
        P("sec", None, None, None),
        P(),
    )
    out_specs = (P("sec", "el", None, None, None), P("sec", "el", None, None, None))
    return jax.shard_map(
        functools.partial(on_device, mesh.shape["sec"], mesh.shape["el"]),
        mesh=mesh,
        in_specs=in_specs,
        out_specs=out_specs,
        check_vma=False,
    )
```

```python
import functools

import jax
import jax.numpy as jnp
import numpy as np
from jax import lax
from jax.experimental import pallas as pl
from jax.experimental.pallas import tpu as pltpu
from jax.sharding import PartitionSpec as P

TR = 8
TC = 16
VMEM_LIMIT = 40 * 1024 * 1024
GROUPS = 4
BATCHES = 2
STEPS = 4
LEADS = (1, 1, 4)


def tables(energies):
    length = energies
    depth = energies // 2
    order = np.concatenate([np.arange(0, length, 2), np.arange(1, length, 2)])
    phase = np.outer(order, np.arange(depth)) % length
    phase = phase * (2.0 * np.pi / length)
    cosine = np.cos(phase).astype(np.float32)
    sine = np.sin(phase).astype(np.float32)
    real = np.stack([cosine, sine], axis=2).reshape(length, length)
    imag = np.stack([-sine, cosine], axis=2).reshape(length, length)
    forward = np.concatenate([real, imag], axis=0)
    out_r = np.concatenate([-sine.T, -cosine.T], axis=1)
    out_i = np.concatenate([cosine.T, -sine.T], axis=1)
    inverse = np.stack([out_r, out_i], axis=1).reshape(length, 2 * length)
    return jnp.asarray(forward, jnp.bfloat16), jnp.asarray(inverse, jnp.bfloat16)


def dot32(a, b):
    return jnp.dot(a, b, preferred_element_type=jnp.float32)


def conjugate_product(a, b):
    (ar, ai), (br, bi) = a, b
    return jnp.concatenate([ar * br + ai * bi, ai * br - ar * bi], axis=0).astype(jnp.bfloat16)


def spectra(parts, forward_ref):
    depth, _, width = parts[0].shape
    length = 2 * depth
    joined = jnp.concatenate([p.reshape(length, width) for p in parts], axis=1)
    z = dot32(forward_ref[...], joined)
    return [
        (z[:length, i * width : (i + 1) * width], z[length:, i * width : (i + 1) * width])
        for i in range(len(parts))
    ]


def low_part(factor, lesser, greater, forward_ref, inverse_ref):
    first, second = spectra([lesser, greater], forward_ref)
    return dot32(inverse_ref[...], conjugate_product(first, second)) * factor


def high_parts(factor, lesser, below, greater, forward_ref, inverse_ref):
    width = lesser.shape[-1]
    first, under, second = spectra([lesser, below, greater], forward_ref)
    middle = under[0].shape[0] // 2

    def shifted(a, b):
        return jnp.concatenate([b[:middle] + a[:middle], b[middle:] - a[middle:]], axis=0)

    both = tuple(shifted(a, b) for a, b in zip(under, second))
    product = jnp.concatenate(
        [conjugate_product(first, both), conjugate_product(first, under)], axis=1
    )
    series = dot32(inverse_ref[...], product) * factor
    return series[:, :width], series[:, width:]


def exchange_kernel(
    owners,
    sections,
    factor,
    lesser_ref,
    greater_ref,
    coulomb_ref,
    forward_hbm,
    inverse_hbm,
    pattern_hbm,
    *refs,
):
    sides = 1 if sections == 2 else 2
    polar_ref = refs[0]
    beside_refs = refs[1 : 1 + sides]
    sum_ref, right_ref, picked_last_ref, mask_last_ref = refs[1 + sides : 5 + sides]
    (
        pattern_ref,
        forward_ref,
        inverse_ref,
        table_sem,
        other_ref,
        coulomb_near,
        picked_ref,
        mask_ref,
        rows_ref,
        near_sem,
        x_ref,
        below_ref,
        down_ref,
        partial_ref,
        d_ref,
        in_send,
        in_recv,
        pass_send,
        pass_recv,
        up_send,
        up_recv,
        down_send,
        down_recv,
        out_send,
        out_recv,
        side_send,
        side_recv,
        c_send,
        c_recv,
    ) = refs[5 + sides :]
    tiles = x_ref.shape[1]
    local = polar_ref.shape[0]
    slots = tiles // GROUPS
    some = local // BATCHES
    group = owners // 4
    half = owners // 2
    me = lax.axis_index("el")
    section = lax.axis_index("sec")
    quarter = me // group
    place = lax.rem(me, group)
    base = quarter * group
    half_base = (quarter // 2) * half
    spot = lax.rem(me, half)
    outer = jnp.logical_or(quarter == 0, quarter == 3)
    inward = jnp.where(quarter == 0, me + group, me - group)
    mesh_id = pl.DeviceIdType.MESH
    if sections == 2:
        targets = [1 - section]
    else:
        targets = [
            lax.rem(section + 1, sections),
            lax.rem(section + sections - 1, sections),
        ]

    load_f = pltpu.make_async_copy(forward_hbm, forward_ref, table_sem.at[0])
    load_i = pltpu.make_async_copy(inverse_hbm, inverse_ref, table_sem.at[1])
    load_p = pltpu.make_async_copy(pattern_hbm, pattern_ref, table_sem.at[2])
    load_f.start()
    load_i.start()
    load_p.start()
    barrier = pltpu.get_barrier_semaphore()

    def greet(step, carry):
        peer = half_base + lax.rem(spot + step, half)
        pl.semaphore_signal(barrier, inc=1, device_id={"el": peer}, device_id_type=mesh_id)
        return carry

    lax.fori_loop(1, half, greet, 0)
    for target in targets:
        pl.semaphore_signal(barrier, inc=1, device_id={"sec": target}, device_id_type=mesh_id)

    @pl.when(quarter < 2)
    def _():
        for peer in range(group):
            pl.semaphore_signal(
                barrier, inc=1, device_id={"el": half + peer}, device_id_type=mesh_id
            )

    @pl.when(quarter == 2)
    def _():
        pl.semaphore_signal(barrier, inc=1, device_id={"el": me - group}, device_id_type=mesh_id)

    greeted = jnp.where(quarter == 2, half, jnp.where(quarter == 1, 1, 0))
    pl.semaphore_wait(barrier, half - 1 + sides + greeted)

    mine = pl.ds(spot * local, local)
    own = pl.ds(lax.rem(quarter, 2) * group * local, group * local)
    theirs = pl.ds((1 - lax.rem(quarter, 2)) * group * local, group * local)

    def send_in(which, source, tile):
        pltpu.make_async_copy(
            source.at[:, place, tile], x_ref.at[which, tile, mine], in_recv.at[which, tile]
        ).start()

        def send(turn, carry):
            peer = lax.rem(place + 1 + turn, group)
            pltpu.make_async_remote_copy(
                src_ref=source.at[:, peer, tile],
                dst_ref=x_ref.at[which, tile, mine],
                send_sem=in_send,
                recv_sem=in_recv.at[which, tile],
                device_id={"el": base + peer},
                device_id_type=mesh_id,
            ).start()
            return carry

        for turn in range(group - 1):
            send(turn, 0)

    def send_both(tile, carry):
        send_in(1, greater_ref, tile)
        send_in(0, lesser_ref, tile)
        return carry

    lax.fori_loop(0, tiles, send_both, 0)

    shared = pltpu.make_async_remote_copy(
        src_ref=coulomb_ref.at[1],
        dst_ref=other_ref,
        send_sem=c_send,
        recv_sem=c_recv,
        device_id={"sec": targets[0]},
        device_id_type=mesh_id,
    )
    shared.start()

    def gathered(which, tile):
        part = x_ref.at[which, tile, own]
        pltpu.make_async_copy(part, part, in_recv.at[which, tile]).wait()

    def pass_inward(which, tile, peer):
        gathered(which, tile)
        pltpu.make_async_remote_copy(
            src_ref=x_ref.at[which, tile, own],
            dst_ref=x_ref.at[which, tile, own],
            send_sem=pass_send,
            recv_sem=pass_recv.at[which, tile],
            device_id={"el": peer},
            device_id_type=mesh_id,
        ).start()

    def passed(which, tile):
        part = x_ref.at[which, tile, theirs]
        pltpu.make_async_copy(part, part, pass_recv.at[which, tile]).wait()

    def forward_copy(tile, side):
        return pltpu.make_async_remote_copy(
            src_ref=polar_ref.at[:, :, tile],
            dst_ref=beside_refs[side].at[:, :, tile],
            send_sem=side_send.at[side, tile],
            recv_sem=side_recv.at[side, tile],
            device_id={"sec": targets[side]},
            device_id_type=mesh_id,
        )

    def pass_on(tile):
        whole = polar_ref.at[:, :, tile]
        pltpu.make_async_copy(whole, whole, out_recv.at[tile]).wait()

        @pl.when(quarter < 2)
        def _():
            part = partial_ref.at[:, :, tile]
            pltpu.make_async_copy(part, part, down_recv.at[tile]).wait()
            both = polar_ref[:, :, tile].astype(jnp.float32)
            both = both + partial_ref[:, :, tile].astype(jnp.float32)
            polar_ref[:, :, tile] = both.astype(jnp.bfloat16)

        for side in range(sides):
            forward_copy(tile, side).start()

    def give(tile):
        pltpu.make_async_copy(
            d_ref.at[tile, mine], polar_ref.at[:, place, tile], out_recv.at[tile]
        ).start()

        def send(turn, carry):
            peer = lax.rem(spot + 1 + turn, half)
            pltpu.make_async_remote_copy(
                src_ref=d_ref.at[tile, pl.ds(peer * local, local)],
                dst_ref=polar_ref.at[:, place, tile],
                send_sem=out_send,
                recv_sem=out_recv.at[tile],
                device_id={"el": half_base + peer},
                device_id_type=mesh_id,
            ).start()
            return carry

        for turn in range(half - 1):
            send(turn, 0)

    def lift(tile):
        gathered(1, tile)
        passed(1, tile)
        pltpu.make_async_remote_copy(
            src_ref=x_ref.at[1, tile],
            dst_ref=below_ref.at[tile],
            send_sem=up_send,
            recv_sem=up_recv.at[tile],
            device_id={"el": me + group},
            device_id_type=mesh_id,
        ).start()
        gathered(0, tile)
        passed(0, tile)
        value = low_part(factor, x_ref[0, tile], x_ref[1, tile], forward_ref, inverse_ref)
        d_ref[tile] = value.astype(jnp.bfloat16).reshape(d_ref.shape[1:])
        give(tile)

    def upper(tile):
        gathered(0, tile)
        gathered(1, tile)
        passed(0, tile)
        passed(1, tile)
        part = below_ref.at[tile]
        pltpu.make_async_copy(part, part, up_recv.at[tile]).wait()
        down, above = high_parts(
            factor, x_ref[0, tile], below_ref[tile], x_ref[1, tile], forward_ref, inverse_ref
        )
        shape = d_ref.shape[1:]
        down_ref[tile] = down.astype(jnp.bfloat16).reshape(shape)
        for peer in range(half):
            pltpu.make_async_remote_copy(
                src_ref=down_ref.at[tile, peer * local : (peer + 1) * local],
                dst_ref=partial_ref.at[:, place, tile],
                send_sem=down_send,
                recv_sem=down_recv.at[tile],
                device_id={"el": peer},
                device_id_type=mesh_id,
            ).start()
        d_ref[tile] = above.astype(jnp.bfloat16).reshape(shape)
        give(tile)

    def prepare():
        pltpu.make_async_copy(coulomb_ref, coulomb_near, near_sem).wait()
        shared.wait_recv()
        screen_setup(
            sections,
            coulomb_near,
            other_ref,
            pattern_ref,
            right_ref,
            picked_ref,
            mask_ref,
            tiles,
        )
        picked_last_ref[...] = picked_ref[GROUPS - 1]
        mask_last_ref[...] = mask_ref[GROUPS - 1]
        for b in range(local):
            sum_ref[b] = jnp.zeros(sum_ref.shape[1:], sum_ref.dtype)

    def screen_some(turn):
        chunk = turn // BATCHES
        batch = lax.rem(turn, BATCHES)

        @pl.when(batch == 0)
        def _():
            for s in range(slots):
                for side in range(sides):
                    forward_copy(chunk * slots + s, side).wait_recv()

        start = batch * some
        columns = pl.ds(chunk * slots, slots)
        sources = [polar_ref, *beside_refs]
        for t in range(1 + sides):
            for b in range(some):
                piece = sources[t][start + b, :, columns]
                rows_ref[t, b] = piece.reshape(rows_ref.shape[2:]).astype(jnp.float32)
        masks = [mask_ref[chunk, t] for t in range(1 + sides)]
        added = screen_chunk(some, rows_ref, masks, right_ref, picked_ref[chunk])
        for b in range(some):
            for c in range(2):
                old = sum_ref[start + b, c].astype(jnp.float32)
                sum_ref[start + b, c] = (old + added[2 * b + c]).astype(jnp.bfloat16)

    pltpu.make_async_copy(coulomb_ref, coulomb_near, near_sem).start()
    load_f.wait()
    load_i.wait()
    load_p.wait()
    turns = (GROUPS - 1) * BATCHES
    stride = max(1, slots // BATCHES)
    behind = 6
    delay = jnp.where(outer, tiles, jnp.where(quarter == 1, behind, 3))
    lead = slots + jnp.where(outer, LEADS[0], jnp.where(quarter == 1, LEADS[1], LEADS[2]))
    last = jnp.maximum(tiles, (turns - 1) * stride + 1 + lead)
    ready = jnp.where(outer, tiles, jnp.where(quarter == 1, 3, 0))

    def body(i, carry):
        @pl.when(jnp.logical_and(outer, i < tiles))
        def _():
            pass_inward(1, i, inward)
            pass_inward(0, i, inward)

        @pl.when(jnp.logical_and(quarter == 1, i < tiles))
        def _():
            lift(i)

        @pl.when(i == ready)
        def _():
            prepare()

        @pl.when(jnp.logical_and(quarter == 2, i < tiles))
        def _():
            upper(i)

        tile = i - delay

        @pl.when(jnp.logical_and(tile >= 0, tile < tiles))
        def _():
            pass_on(tile)

        since = tile - lead
        turn = since // stride

        @pl.when(
            jnp.logical_and(since >= 0, jnp.logical_and(since % stride == 0, turn < turns))
        )
        def _():
            screen_some(turn)

        return carry

    lax.fori_loop(0, last + delay, body, 0)

    @pl.when(outer)
    def _():
        part = x_ref.at[:, :, own]
        pltpu.make_async_copy(part, part, pass_send).wait()

    @pl.when(jnp.logical_not(outer))
    def _():
        part = d_ref.at[:, pl.ds(0, (half - 1) * local)]
        pltpu.make_async_copy(part, part, out_send).wait()

    @pl.when(quarter == 1)
    def _():
        pltpu.make_async_copy(below_ref, below_ref, up_send).wait()

    @pl.when(quarter == 2)
    def _():
        pltpu.make_async_copy(down_ref, down_ref, down_send).wait()

    part = x_ref.at[:, :, pl.ds(0, (group - 1) * local)]
    pltpu.make_async_copy(part, part, in_send).wait()

    def settle_sent(tile, carry):
        for side in range(sides):
            forward_copy(tile, side).wait_send()
        return carry

    def settle(tile, carry):
        for side in range(sides):
            forward_copy(tile, side).wait()
        return carry

    lax.fori_loop(0, (GROUPS - 1) * slots, settle_sent, 0)
    lax.fori_loop((GROUPS - 1) * slots, tiles, settle, 0)
    shared.wait_send()


def exchange(owners, sections, lesser, greater, coulomb, pattern):
    local, count, _, width = lesser.shape
    group = owners // 4
    tiles = count // group
    energies = local * owners
    depth = energies // 2
    nb = coulomb.shape[1]
    sides = 1 if sections == 2 else 2
    terms = 1 + sides
    chunk = count // GROUPS
    forward, inverse = tables(energies)
    split = (local, group, tiles, 2, width)
    bf16 = jnp.bfloat16
    far = pl.BlockSpec(memory_space=pltpu.HBM)
    near = pl.BlockSpec(memory_space=pltpu.VMEM)
    dma = pltpu.SemaphoreType.DMA
    buffer = pltpu.VMEM((tiles, depth, 2, width), bf16)
    operands = [lesser.reshape(split), greater.reshape(split), coulomb, forward, inverse, pattern]
    return pl.pallas_call(
        functools.partial(exchange_kernel, owners, sections, 1.0 / (energies * energies**0.5)),
        in_specs=[far] * 6,
        out_specs=[near] * (5 + sides),
        out_shape=[pltpu.VMEM(split, bf16)] * (1 + sides)
        + [
            pltpu.VMEM((local, 2, nb, nb), bf16),
            pltpu.VMEM((terms, nb, nb), bf16),
            pltpu.VMEM((nb, terms * TR * chunk), bf16),
            pltpu.VMEM((terms, chunk, nb), bf16),
        ],
        scratch_shapes=[
            pltpu.VMEM(pattern.shape, pattern.dtype),
            pltpu.VMEM(forward.shape, bf16),
            pltpu.VMEM(inverse.shape, bf16),
            dma((3,)),
            pltpu.VMEM((nb, nb), bf16),
            pltpu.VMEM(coulomb.shape, bf16),
            pltpu.VMEM((GROUPS, nb, terms * TR * chunk), bf16),
            pltpu.VMEM((GROUPS, terms, chunk, nb), bf16),
            pltpu.VMEM((terms, local // BATCHES, 2 * chunk, width), jnp.float32),
            dma(()),
            pltpu.VMEM((2, tiles, depth, 2, width), bf16),
            buffer,
            buffer,
            pltpu.VMEM(split, bf16),
            buffer,
            dma(()),
            dma((2, tiles)),
            dma(()),
            dma((2, tiles)),
            dma(()),
            dma((tiles,)),
            dma(()),
            dma((tiles,)),
            dma(()),
            dma((tiles,)),
            dma((sides, tiles)),
            dma((sides, tiles)),
            dma(()),
            dma(()),
        ],
        compiler_params=pltpu.CompilerParams(
            collective_id=0, has_side_effects=True, vmem_limit_bytes=VMEM_LIMIT
        ),
    )(*[pltpu.with_memory_space_constraint(array, pltpu.HBM) for array in operands])


def screen_setup(
    sections, coulomb_ref, other_ref, pattern_ref, right_ref, picked_ref, mask_ref, tiles
):
    groups, terms, chunk, nb = mask_ref.shape
    count = groups * chunk
    slots = tiles // groups
    section = lax.axis_index("sec")
    lower = other_ref[...].astype(jnp.float32).T
    upper = coulomb_ref[1].astype(jnp.float32)
    matrices = [coulomb_ref[0].astype(jnp.float32)]
    if sections == 2:
        sources = [section, 1 - section]
        matrices.append(jnp.where(section == 0, upper, lower))
    else:
        sources = [
            section,
            lax.rem(section + sections - 1, sections),
            lax.rem(section + 1, sections),
        ]
        matrices.append(jnp.where(section > 0, lower, 0.0))
        matrices.append(jnp.where(section < sections - 1, upper, 0.0))
    across = nb // TC
    wide = TR * count
    iota = lambda shape, axis: lax.broadcasted_iota(jnp.int32, shape, axis)
    row_of = iota((nb, wide), 0)
    lane = iota((count, wide), 1)
    member = lane % chunk
    listed_at = (member // slots) * tiles + lane // (TR * chunk) * slots + member % slots
    taken = listed_at == iota((count, wide), 0)
    inner_row = iota((1, wide), 1) // chunk % TR
    diagonal = iota((count, count), 0) == iota((count, count), 1)
    member = iota((chunk, count), 0)
    begin = (member // slots) * tiles + member % slots
    column_of = iota((chunk, nb), 1) // TC
    for t in range(terms):
        listed = pattern_ref[pl.ds(sources[t], 1), :].astype(jnp.float32)
        upright = jnp.sum(jnp.where(diagonal, listed, 0.0), axis=1, keepdims=True)
        spread = jnp.sum(jnp.where(taken, upright, 0.0), axis=0, keepdims=True).astype(jnp.int32)
        row = spread // across * TR + inner_row
        chosen = jnp.where(row_of == row, 1.0, 0.0).astype(jnp.bfloat16)
        picked = dot32(matrices[t].astype(jnp.bfloat16), chosen).astype(jnp.bfloat16)
        span = TR * chunk
        for g in range(groups):
            picked_ref[g, :, t * span : (t + 1) * span] = picked[:, g * span : (g + 1) * span]
            here = iota((chunk, count), 1) == begin + g * slots
            place = jnp.sum(jnp.where(here, listed, 0.0), axis=1, keepdims=True).astype(jnp.int32)
            mask_ref[g, t] = jnp.where(column_of == place % across, 1.0, 0.0).astype(jnp.bfloat16)
        right_ref[t] = matrices[t].T.astype(jnp.bfloat16)


def right_part(batch, rows, mask, right):
    chunk, nb = mask.shape
    width = rows.shape[-1]
    lane = lax.broadcasted_iota(jnp.int32, (chunk, width), 1) % TC
    stacked = []
    for b in range(batch):
        for c in range(2):
            tile = rows[b, pl.ds(c, chunk, stride=2), :]
            for r in range(TR):
                spread = jnp.take_along_axis(
                    tile, lane + r * TC, axis=1, mode="promise_in_bounds"
                ).astype(jnp.bfloat16)
                stacked.append(jnp.concatenate([spread] * (nb // width), axis=1) * mask)
    return dot32(jnp.concatenate(stacked, axis=0), right).astype(jnp.bfloat16)


def screen_chunk(batch, rows_ref, masks, right_ref, picked):
    span = TR * masks[0].shape[0]
    halves = [
        right_part(batch, rows_ref.at[t], mask, right_ref[t]) for t, mask in enumerate(masks)
    ]
    added = []
    for n in range(2 * batch):
        part = jnp.concatenate([h[n * span : (n + 1) * span] for h in halves], axis=0)
        added.append(dot32(picked, part))
    return added


def screen_kernel(terms, batch, *refs):
    tile_refs = refs[:terms]
    sum_ref, right_ref, picked_ref, mask_ref, polar_out, out_hbm = refs[terms : terms + 6]
    total_ref, rows_ref, half_ref, keep_sem, total_sem = refs[terms + 6 :]
    polar_ref = tile_refs[0]
    local, _, per, _, _ = polar_ref.shape
    slots = per // GROUPS
    steps = local // batch
    def store(step):
        part = pl.ds(step * batch, batch)
        return pltpu.make_async_copy(total_ref.at[part], out_hbm.at[part], total_sem.at[step])

    keep = pltpu.make_async_copy(polar_ref, polar_out, keep_sem)
    keep.start()
    masks = [mask_ref[t] for t in range(terms)]

    span = TR * mask_ref.shape[1]
    wide = local // max(1, local // 16)

    def fill(step, carry):
        for t in range(terms):
            for b in range(wide):
                e = step * wide + b
                piece = tile_refs[t][e, :, per - slots :]
                rows_ref[t, b] = piece.reshape(rows_ref.shape[2:]).astype(jnp.float32)
            half = right_part(wide, rows_ref.at[t], masks[t], right_ref[t])
            half_ref[pl.ds(step * wide * 2, wide * 2), t * span : (t + 1) * span] = half.reshape(
                wide * 2, span, half.shape[-1]
            )
        return carry

    lax.fori_loop(0, local // wide, fill, 0)

    def body(step, carry):
        for b in range(batch):
            for c in range(2):
                e = step * batch + b
                total = dot32(picked_ref[...], half_ref[2 * e + c])
                total = total + sum_ref[e, c].astype(jnp.float32)
                total_ref[e, c] = total.astype(jnp.bfloat16)
        store(step).start()
        return carry

    for step in range(steps):
        body(step, 0)
    keep.wait()
    for step in range(steps):
        store(step).wait()


def screen(tiles, total, right, picked, mask):
    terms = len(tiles)
    local, _, _, _, width = tiles[0].shape
    chunk = mask.shape[1]
    batch = max(1, local // STEPS)
    dma = pltpu.SemaphoreType.DMA
    return pl.pallas_call(
        functools.partial(screen_kernel, terms, batch),
        in_specs=[pl.BlockSpec(memory_space=pltpu.VMEM)] * (terms + 4),
        out_specs=[pl.BlockSpec(memory_space=pltpu.HBM)] * 2,
        out_shape=[
            jax.ShapeDtypeStruct(tiles[0].shape, jnp.bfloat16),
            jax.ShapeDtypeStruct(total.shape, total.dtype),
        ],
        scratch_shapes=[
            pltpu.VMEM(total.shape, total.dtype),
            pltpu.VMEM((terms, local, 2 * chunk, width), jnp.float32),
            pltpu.VMEM((2 * local, terms * TR * chunk, total.shape[-1]), jnp.bfloat16),
            dma(()),
            dma((local // batch,)),
        ],
        compiler_params=pltpu.CompilerParams(vmem_limit_bytes=VMEM_LIMIT),
    )(*tiles, total, right, picked, mask)


def on_device(sections, owners, green_lesser, green_greater, coulomb, pattern):
    _, local, count, _, width = green_lesser.shape
    sides = 1 if sections == 2 else 2
    results = exchange(
        owners, sections, green_lesser[0], green_greater[0], coulomb[0], pattern
    )
    polar, screened = screen(results[: 1 + sides], *results[1 + sides :])
    return polar.reshape(1, local, count, 2, width), screened[None]


def solution(mesh):
    in_specs = (
        P("sec", "el", None, None, None),
        P("sec", "el", None, None, None),
        P("sec", None, None, None),
        P(),
    )
    out_specs = (P("sec", "el", None, None, None), P("sec", "el", None, None, None))
    return jax.shard_map(
        functools.partial(on_device, mesh.shape["sec"], mesh.shape["el"]),
        mesh=mesh,
        in_specs=in_specs,
        out_specs=out_specs,
        check_vma=False,
    )
```

```python
import functools

import jax
import jax.numpy as jnp
import numpy as np
from jax import lax
from jax.experimental import pallas as pl
from jax.experimental.pallas import tpu as pltpu
from jax.sharding import PartitionSpec as P

TR = 8
TC = 16
VMEM_LIMIT = 40 * 1024 * 1024
GROUPS = 4
BATCHES = 2
STEPS = 8
LEADS = (1, 1, 4)


def tables(energies):
    length = energies
    depth = energies // 2
    order = np.concatenate([np.arange(0, length, 2), np.arange(1, length, 2)])
    phase = np.outer(order, np.arange(depth)) % length
    phase = phase * (2.0 * np.pi / length)
    cosine = np.cos(phase).astype(np.float32)
    sine = np.sin(phase).astype(np.float32)
    real = np.stack([cosine, sine], axis=2).reshape(length, length)
    imag = np.stack([-sine, cosine], axis=2).reshape(length, length)
    forward = np.concatenate([real, imag], axis=0)
    out_r = np.concatenate([-sine.T, -cosine.T], axis=1)
    out_i = np.concatenate([cosine.T, -sine.T], axis=1)
    inverse = np.stack([out_r, out_i], axis=1).reshape(length, 2 * length)
    return jnp.asarray(forward, jnp.bfloat16), jnp.asarray(inverse, jnp.bfloat16)


def dot32(a, b):
    return jnp.dot(a, b, preferred_element_type=jnp.float32)


def conjugate_product(a, b):
    (ar, ai), (br, bi) = a, b
    return jnp.concatenate([ar * br + ai * bi, ai * br - ar * bi], axis=0).astype(jnp.bfloat16)


def spectra(parts, forward_ref):
    depth, _, width = parts[0].shape
    length = 2 * depth
    joined = jnp.concatenate([p.reshape(length, width) for p in parts], axis=1)
    z = dot32(forward_ref[...], joined)
    return [
        (z[:length, i * width : (i + 1) * width], z[length:, i * width : (i + 1) * width])
        for i in range(len(parts))
    ]


def low_part(factor, lesser, greater, forward_ref, inverse_ref):
    first, second = spectra([lesser, greater], forward_ref)
    return dot32(inverse_ref[...], conjugate_product(first, second)) * factor


def high_parts(factor, lesser, below, greater, forward_ref, inverse_ref):
    width = lesser.shape[-1]
    first, under, second = spectra([lesser, below, greater], forward_ref)
    middle = under[0].shape[0] // 2

    def shifted(a, b):
        return jnp.concatenate([b[:middle] + a[:middle], b[middle:] - a[middle:]], axis=0)

    both = tuple(shifted(a, b) for a, b in zip(under, second))
    product = jnp.concatenate(
        [conjugate_product(first, both), conjugate_product(first, under)], axis=1
    )
    series = dot32(inverse_ref[...], product) * factor
    return series[:, :width], series[:, width:]


def exchange_kernel(
    owners,
    sections,
    factor,
    lesser_ref,
    greater_ref,
    coulomb_ref,
    forward_hbm,
    inverse_hbm,
    pattern_hbm,
    *refs,
):
    sides = 1 if sections == 2 else 2
    polar_ref = refs[0]
    beside_refs = refs[1 : 1 + sides]
    sum_ref, right_ref, picked_last_ref, mask_last_ref, ours_ref = refs[1 + sides : 6 + sides]
    (
        pattern_ref,
        last_ref,
        forward_ref,
        inverse_ref,
        table_sem,
        other_ref,
        coulomb_near,
        picked_ref,
        mask_ref,
        rows_ref,
        near_sem,
        x_ref,
        below_ref,
        down_ref,
        partial_ref,
        d_ref,
        in_send,
        in_recv,
        pass_send,
        pass_recv,
        up_send,
        up_recv,
        down_send,
        down_recv,
        out_send,
        out_recv,
        side_send,
        side_recv,
        c_send,
        c_recv,
    ) = refs[6 + sides :]
    tiles = x_ref.shape[1]
    local = polar_ref.shape[0]
    slots = tiles // GROUPS
    some = local // BATCHES
    group = owners // 4
    half = owners // 2
    me = lax.axis_index("el")
    section = lax.axis_index("sec")
    quarter = me // group
    place = lax.rem(me, group)
    base = quarter * group
    half_base = (quarter // 2) * half
    spot = lax.rem(me, half)
    outer = jnp.logical_or(quarter == 0, quarter == 3)
    inward = jnp.where(quarter == 0, me + group, me - group)
    mesh_id = pl.DeviceIdType.MESH
    if sections == 2:
        targets = [1 - section]
    else:
        targets = [
            lax.rem(section + 1, sections),
            lax.rem(section + sections - 1, sections),
        ]

    load_f = pltpu.make_async_copy(forward_hbm, forward_ref, table_sem.at[0])
    load_i = pltpu.make_async_copy(inverse_hbm, inverse_ref, table_sem.at[1])
    load_p = pltpu.make_async_copy(pattern_hbm, pattern_ref, table_sem.at[2])
    load_f.start()
    load_i.start()
    load_p.start()
    barrier = pltpu.get_barrier_semaphore()

    def greet(step, carry):
        peer = half_base + lax.rem(spot + step, half)
        pl.semaphore_signal(barrier, inc=1, device_id={"el": peer}, device_id_type=mesh_id)
        return carry

    lax.fori_loop(1, half, greet, 0)
    for target in targets:
        pl.semaphore_signal(barrier, inc=1, device_id={"sec": target}, device_id_type=mesh_id)

    @pl.when(quarter < 2)
    def _():
        for peer in range(group):
            pl.semaphore_signal(
                barrier, inc=1, device_id={"el": half + peer}, device_id_type=mesh_id
            )

    @pl.when(quarter == 2)
    def _():
        pl.semaphore_signal(barrier, inc=1, device_id={"el": me - group}, device_id_type=mesh_id)

    greeted = jnp.where(quarter == 2, half, jnp.where(quarter == 1, 1, 0))
    pl.semaphore_wait(barrier, half - 1 + sides + greeted)

    mine = pl.ds(spot * local, local)
    own = pl.ds(lax.rem(quarter, 2) * group * local, group * local)
    theirs = pl.ds((1 - lax.rem(quarter, 2)) * group * local, group * local)

    def send_in(which, source, tile):
        pltpu.make_async_copy(
            source.at[:, place, tile], x_ref.at[which, tile, mine], in_recv.at[which, tile]
        ).start()

        def send(turn, carry):
            peer = lax.rem(place + 1 + turn, group)
            pltpu.make_async_remote_copy(
                src_ref=source.at[:, peer, tile],
                dst_ref=x_ref.at[which, tile, mine],
                send_sem=in_send,
                recv_sem=in_recv.at[which, tile],
                device_id={"el": base + peer},
                device_id_type=mesh_id,
            ).start()
            return carry

        for turn in range(group - 1):
            send(turn, 0)

    def send_both(tile, carry):
        send_in(1, greater_ref, tile)
        send_in(0, lesser_ref, tile)
        return carry

    lax.fori_loop(0, tiles, send_both, 0)

    shared = pltpu.make_async_remote_copy(
        src_ref=coulomb_ref.at[1],
        dst_ref=other_ref,
        send_sem=c_send,
        recv_sem=c_recv,
        device_id={"sec": targets[0]},
        device_id_type=mesh_id,
    )
    shared.start()

    def gathered(which, tile):
        part = x_ref.at[which, tile, own]
        pltpu.make_async_copy(part, part, in_recv.at[which, tile]).wait()

    def pass_inward(which, tile, peer):
        gathered(which, tile)
        pltpu.make_async_remote_copy(
            src_ref=x_ref.at[which, tile, own],
            dst_ref=x_ref.at[which, tile, own],
            send_sem=pass_send,
            recv_sem=pass_recv.at[which, tile],
            device_id={"el": peer},
            device_id_type=mesh_id,
        ).start()

    def passed(which, tile):
        part = x_ref.at[which, tile, theirs]
        pltpu.make_async_copy(part, part, pass_recv.at[which, tile]).wait()

    def forward_copy(tile, side):
        return pltpu.make_async_remote_copy(
            src_ref=polar_ref.at[:, :, tile],
            dst_ref=beside_refs[side].at[:, :, tile],
            send_sem=side_send.at[side, tile],
            recv_sem=side_recv.at[side, tile],
            device_id={"sec": targets[side]},
            device_id_type=mesh_id,
        )

    def pass_on(tile):
        whole = polar_ref.at[:, :, tile]
        pltpu.make_async_copy(whole, whole, out_recv.at[tile]).wait()

        @pl.when(quarter < 2)
        def _():
            part = partial_ref.at[:, :, tile]
            pltpu.make_async_copy(part, part, down_recv.at[tile]).wait()
            both = polar_ref[:, :, tile].astype(jnp.float32)
            both = both + partial_ref[:, :, tile].astype(jnp.float32)
            polar_ref[:, :, tile] = both.astype(jnp.bfloat16)

        for side in range(sides):
            forward_copy(tile, side).start()

    def give(tile):
        pltpu.make_async_copy(
            d_ref.at[tile, mine], polar_ref.at[:, place, tile], out_recv.at[tile]
        ).start()

        def send(turn, carry):
            peer = lax.rem(spot + 1 + turn, half)
            pltpu.make_async_remote_copy(
                src_ref=d_ref.at[tile, pl.ds(peer * local, local)],
                dst_ref=polar_ref.at[:, place, tile],
                send_sem=out_send,
                recv_sem=out_recv.at[tile],
                device_id={"el": half_base + peer},
                device_id_type=mesh_id,
            ).start()
            return carry

        for turn in range(half - 1):
            send(turn, 0)

    def lift(tile):
        gathered(1, tile)
        passed(1, tile)
        pltpu.make_async_remote_copy(
            src_ref=x_ref.at[1, tile],
            dst_ref=below_ref.at[tile],
            send_sem=up_send,
            recv_sem=up_recv.at[tile],
            device_id={"el": me + group},
            device_id_type=mesh_id,
        ).start()
        gathered(0, tile)
        passed(0, tile)
        value = low_part(factor, x_ref[0, tile], x_ref[1, tile], forward_ref, inverse_ref)
        d_ref[tile] = value.astype(jnp.bfloat16).reshape(d_ref.shape[1:])
        give(tile)

    def upper(tile):
        gathered(0, tile)
        gathered(1, tile)
        passed(0, tile)
        passed(1, tile)
        part = below_ref.at[tile]
        pltpu.make_async_copy(part, part, up_recv.at[tile]).wait()
        down, above = high_parts(
            factor, x_ref[0, tile], below_ref[tile], x_ref[1, tile], forward_ref, inverse_ref
        )
        shape = d_ref.shape[1:]
        down_ref[tile] = down.astype(jnp.bfloat16).reshape(shape)
        for peer in range(half):
            pltpu.make_async_remote_copy(
                src_ref=down_ref.at[tile, peer * local : (peer + 1) * local],
                dst_ref=partial_ref.at[:, place, tile],
                send_sem=down_send,
                recv_sem=down_recv.at[tile],
                device_id={"el": peer},
                device_id_type=mesh_id,
            ).start()
        d_ref[tile] = above.astype(jnp.bfloat16).reshape(shape)
        give(tile)

    def prepare():
        pltpu.make_async_copy(coulomb_ref, coulomb_near, near_sem).wait()
        shared.wait_recv()
        screen_setup(
            sections,
            coulomb_near,
            other_ref,
            pattern_ref,
            right_ref,
            picked_ref,
            mask_ref,
            tiles,
        )
        picked_last_ref[...] = picked_ref[GROUPS - 1]
        mask_last_ref[...] = mask_ref[GROUPS - 1]
        for b in range(local):
            sum_ref[b] = jnp.zeros(sum_ref.shape[1:], sum_ref.dtype)

    def screen_some(turn):
        chunk = turn // BATCHES
        batch = lax.rem(turn, BATCHES)

        @pl.when(batch == 0)
        def _():
            for s in range(slots):
                for side in range(sides):
                    forward_copy(chunk * slots + s, side).wait_recv()

        start = batch * some
        columns = pl.ds(chunk * slots, slots)
        sources = [polar_ref, *beside_refs]
        for t in range(1 + sides):
            for b in range(some):
                piece = sources[t][start + b, :, columns]
                rows_ref[t, b] = piece.reshape(rows_ref.shape[2:]).astype(jnp.float32)
        masks = [mask_ref[chunk, t] for t in range(1 + sides)]
        added = screen_chunk(some, rows_ref, masks, right_ref, picked_ref[chunk])
        for b in range(some):
            for c in range(2):
                old = sum_ref[start + b, c].astype(jnp.float32)
                sum_ref[start + b, c] = (old + added[2 * b + c]).astype(jnp.bfloat16)

    pltpu.make_async_copy(coulomb_ref, coulomb_near, near_sem).start()
    load_f.wait()
    load_i.wait()
    load_p.wait()
    turns = (GROUPS - 1) * BATCHES
    stride = max(1, slots // BATCHES)
    behind = 6
    delay = jnp.where(outer, tiles, jnp.where(quarter == 1, behind, 3))
    lead = slots + jnp.where(outer, LEADS[0], jnp.where(quarter == 1, LEADS[1], LEADS[2]))
    last = jnp.maximum(tiles, (turns - 1) * stride + 1 + lead)
    ready = jnp.where(outer, tiles, jnp.where(quarter == 1, 3, 0))

    def body(i, carry):
        @pl.when(jnp.logical_and(outer, i < tiles))
        def _():
            pass_inward(1, i, inward)
            pass_inward(0, i, inward)

        @pl.when(jnp.logical_and(quarter == 1, i < tiles))
        def _():
            lift(i)

        @pl.when(i == ready)
        def _():
            prepare()

        @pl.when(jnp.logical_and(quarter == 2, i < tiles))
        def _():
            upper(i)

        tile = i - delay

        @pl.when(jnp.logical_and(tile >= 0, tile < tiles))
        def _():
            pass_on(tile)

        since = tile - lead
        turn = since // stride

        @pl.when(
            jnp.logical_and(since >= 0, jnp.logical_and(since % stride == 0, turn < turns))
        )
        def _():
            screen_some(turn)

        return carry

    lax.fori_loop(0, last + delay, body, 0)
    for b in range(local):
        piece = polar_ref[b, :, tiles - slots :]
        last_ref[b] = piece.reshape(last_ref.shape[1:]).astype(jnp.float32)
    ours = right_part(local, last_ref, mask_ref[GROUPS - 1, 0], right_ref[0])
    ours_ref[...] = ours.reshape(ours_ref.shape)

    @pl.when(outer)
    def _():
        part = x_ref.at[:, :, own]
        pltpu.make_async_copy(part, part, pass_send).wait()

    @pl.when(jnp.logical_not(outer))
    def _():
        part = d_ref.at[:, pl.ds(0, (half - 1) * local)]
        pltpu.make_async_copy(part, part, out_send).wait()

    @pl.when(quarter == 1)
    def _():
        pltpu.make_async_copy(below_ref, below_ref, up_send).wait()

    @pl.when(quarter == 2)
    def _():
        pltpu.make_async_copy(down_ref, down_ref, down_send).wait()

    part = x_ref.at[:, :, pl.ds(0, (group - 1) * local)]
    pltpu.make_async_copy(part, part, in_send).wait()

    def settle_sent(tile, carry):
        for side in range(sides):
            forward_copy(tile, side).wait_send()
        return carry

    def settle(tile, carry):
        for side in range(sides):
            forward_copy(tile, side).wait()
        return carry

    lax.fori_loop(0, (GROUPS - 1) * slots, settle_sent, 0)
    lax.fori_loop((GROUPS - 1) * slots, tiles, settle, 0)
    shared.wait_send()


def exchange(owners, sections, lesser, greater, coulomb, pattern):
    local, count, _, width = lesser.shape
    group = owners // 4
    tiles = count // group
    energies = local * owners
    depth = energies // 2
    nb = coulomb.shape[1]
    sides = 1 if sections == 2 else 2
    terms = 1 + sides
    chunk = count // GROUPS
    forward, inverse = tables(energies)
    split = (local, group, tiles, 2, width)
    bf16 = jnp.bfloat16
    far = pl.BlockSpec(memory_space=pltpu.HBM)
    near = pl.BlockSpec(memory_space=pltpu.VMEM)
    dma = pltpu.SemaphoreType.DMA
    buffer = pltpu.VMEM((tiles, depth, 2, width), bf16)
    operands = [lesser.reshape(split), greater.reshape(split), coulomb, forward, inverse, pattern]
    return pl.pallas_call(
        functools.partial(exchange_kernel, owners, sections, 1.0 / (energies * energies**0.5)),
        in_specs=[far] * 6,
        out_specs=[near] * (6 + sides),
        out_shape=[pltpu.VMEM(split, bf16)] * (1 + sides)
        + [
            pltpu.VMEM((local, 2, nb, nb), bf16),
            pltpu.VMEM((terms, nb, nb), bf16),
            pltpu.VMEM((nb, terms * TR * chunk), bf16),
            pltpu.VMEM((terms, chunk, nb), bf16),
            pltpu.VMEM((2 * local, TR * chunk, nb), bf16),
        ],
        scratch_shapes=[
            pltpu.VMEM(pattern.shape, pattern.dtype),
            pltpu.VMEM((local, 2 * chunk, width), jnp.float32),
            pltpu.VMEM(forward.shape, bf16),
            pltpu.VMEM(inverse.shape, bf16),
            dma((3,)),
            pltpu.VMEM((nb, nb), bf16),
            pltpu.VMEM(coulomb.shape, bf16),
            pltpu.VMEM((GROUPS, nb, terms * TR * chunk), bf16),
            pltpu.VMEM((GROUPS, terms, chunk, nb), bf16),
            pltpu.VMEM((terms, local // BATCHES, 2 * chunk, width), jnp.float32),
            dma(()),
            pltpu.VMEM((2, tiles, depth, 2, width), bf16),
            buffer,
            buffer,
            pltpu.VMEM(split, bf16),
            buffer,
            dma(()),
            dma((2, tiles)),
            dma(()),
            dma((2, tiles)),
            dma(()),
            dma((tiles,)),
            dma(()),
            dma((tiles,)),
            dma(()),
            dma((tiles,)),
            dma((sides, tiles)),
            dma((sides, tiles)),
            dma(()),
            dma(()),
        ],
        compiler_params=pltpu.CompilerParams(
            collective_id=0, has_side_effects=True, vmem_limit_bytes=VMEM_LIMIT
        ),
    )(*[pltpu.with_memory_space_constraint(array, pltpu.HBM) for array in operands])


def screen_setup(
    sections, coulomb_ref, other_ref, pattern_ref, right_ref, picked_ref, mask_ref, tiles
):
    groups, terms, chunk, nb = mask_ref.shape
    count = groups * chunk
    slots = tiles // groups
    section = lax.axis_index("sec")
    lower = other_ref[...].astype(jnp.float32).T
    upper = coulomb_ref[1].astype(jnp.float32)
    matrices = [coulomb_ref[0].astype(jnp.float32)]
    if sections == 2:
        sources = [section, 1 - section]
        matrices.append(jnp.where(section == 0, upper, lower))
    else:
        sources = [
            section,
            lax.rem(section + sections - 1, sections),
            lax.rem(section + 1, sections),
        ]
        matrices.append(jnp.where(section > 0, lower, 0.0))
        matrices.append(jnp.where(section < sections - 1, upper, 0.0))
    across = nb // TC
    wide = TR * count
    iota = lambda shape, axis: lax.broadcasted_iota(jnp.int32, shape, axis)
    row_of = iota((nb, wide), 0)
    lane = iota((count, wide), 1)
    member = lane % chunk
    listed_at = (member // slots) * tiles + lane // (TR * chunk) * slots + member % slots
    taken = listed_at == iota((count, wide), 0)
    inner_row = iota((1, wide), 1) // chunk % TR
    diagonal = iota((count, count), 0) == iota((count, count), 1)
    member = iota((chunk, count), 0)
    begin = (member // slots) * tiles + member % slots
    column_of = iota((chunk, nb), 1) // TC
    for t in range(terms):
        listed = pattern_ref[pl.ds(sources[t], 1), :].astype(jnp.float32)
        upright = jnp.sum(jnp.where(diagonal, listed, 0.0), axis=1, keepdims=True)
        spread = jnp.sum(jnp.where(taken, upright, 0.0), axis=0, keepdims=True).astype(jnp.int32)
        row = spread // across * TR + inner_row
        chosen = jnp.where(row_of == row, 1.0, 0.0).astype(jnp.bfloat16)
        picked = dot32(matrices[t].astype(jnp.bfloat16), chosen).astype(jnp.bfloat16)
        span = TR * chunk
        for g in range(groups):
            picked_ref[g, :, t * span : (t + 1) * span] = picked[:, g * span : (g + 1) * span]
            here = iota((chunk, count), 1) == begin + g * slots
            place = jnp.sum(jnp.where(here, listed, 0.0), axis=1, keepdims=True).astype(jnp.int32)
            mask_ref[g, t] = jnp.where(column_of == place % across, 1.0, 0.0).astype(jnp.bfloat16)
        right_ref[t] = matrices[t].T.astype(jnp.bfloat16)


def right_part(batch, rows, mask, right):
    chunk, nb = mask.shape
    width = rows.shape[-1]
    lane = lax.broadcasted_iota(jnp.int32, (chunk, width), 1) % TC
    stacked = []
    for b in range(batch):
        for c in range(2):
            tile = rows[b, pl.ds(c, chunk, stride=2), :]
            for r in range(TR):
                spread = jnp.take_along_axis(
                    tile, lane + r * TC, axis=1, mode="promise_in_bounds"
                ).astype(jnp.bfloat16)
                stacked.append(jnp.concatenate([spread] * (nb // width), axis=1) * mask)
    return dot32(jnp.concatenate(stacked, axis=0), right).astype(jnp.bfloat16)


def screen_chunk(batch, rows_ref, masks, right_ref, picked):
    span = TR * masks[0].shape[0]
    halves = [
        right_part(batch, rows_ref.at[t], mask, right_ref[t]) for t, mask in enumerate(masks)
    ]
    added = []
    for n in range(2 * batch):
        part = jnp.concatenate([h[n * span : (n + 1) * span] for h in halves], axis=0)
        added.append(dot32(picked, part))
    return added


def screen_kernel(terms, batch, *refs):
    tile_refs = refs[:terms]
    sum_ref, right_ref, picked_ref, mask_ref, ours_ref, polar_out, out_hbm = refs[terms : terms + 7]
    total_ref, rows_ref, half_ref, keep_sem, total_sem = refs[terms + 7 :]
    polar_ref = tile_refs[0]
    local, _, per, _, _ = polar_ref.shape
    slots = per // GROUPS
    steps = local // batch
    def store(step):
        part = pl.ds(step * batch, batch)
        return pltpu.make_async_copy(total_ref.at[part], out_hbm.at[part], total_sem.at[step])

    keep = pltpu.make_async_copy(polar_ref, polar_out, keep_sem)
    keep.start()
    masks = [mask_ref[t] for t in range(terms)]

    span = TR * mask_ref.shape[1]
    wide = local // max(1, local // 16)

    def fill(step, carry):
        for t in range(1, terms):
            for b in range(wide):
                e = step * wide + b
                piece = tile_refs[t][e, :, per - slots :]
                rows_ref[t, b] = piece.reshape(rows_ref.shape[2:]).astype(jnp.float32)
            half = right_part(wide, rows_ref.at[t], masks[t], right_ref[t])
            half_ref[pl.ds(step * wide * 2, wide * 2), (t - 1) * span : t * span] = half.reshape(
                wide * 2, span, half.shape[-1]
            )
        return carry

    lax.fori_loop(0, local // wide, fill, 0)

    def body(step, carry):
        for b in range(batch):
            for c in range(2):
                e = step * batch + b
                part = jnp.concatenate([ours_ref[2 * e + c], half_ref[2 * e + c]], axis=0)
                total = dot32(picked_ref[...], part)
                total = total + sum_ref[e, c].astype(jnp.float32)
                total_ref[e, c] = total.astype(jnp.bfloat16)
        store(step).start()
        return carry

    for step in range(steps):
        body(step, 0)
    keep.wait()
    for step in range(steps):
        store(step).wait()


def screen(tiles, total, right, picked, mask, ours):
    terms = len(tiles)
    local, _, _, _, width = tiles[0].shape
    chunk = mask.shape[1]
    batch = max(1, local // STEPS)
    dma = pltpu.SemaphoreType.DMA
    return pl.pallas_call(
        functools.partial(screen_kernel, terms, batch),
        in_specs=[pl.BlockSpec(memory_space=pltpu.VMEM)] * (terms + 5),
        out_specs=[pl.BlockSpec(memory_space=pltpu.HBM)] * 2,
        out_shape=[
            jax.ShapeDtypeStruct(tiles[0].shape, jnp.bfloat16),
            jax.ShapeDtypeStruct(total.shape, total.dtype),
        ],
        scratch_shapes=[
            pltpu.VMEM(total.shape, total.dtype),
            pltpu.VMEM((terms, local, 2 * chunk, width), jnp.float32),
            pltpu.VMEM((2 * local, (terms - 1) * TR * chunk, total.shape[-1]), jnp.bfloat16),
            dma(()),
            dma((local // batch,)),
        ],
        compiler_params=pltpu.CompilerParams(vmem_limit_bytes=VMEM_LIMIT),
    )(*tiles, total, right, picked, mask, ours)


def on_device(sections, owners, green_lesser, green_greater, coulomb, pattern):
    _, local, count, _, width = green_lesser.shape
    sides = 1 if sections == 2 else 2
    results = exchange(
        owners, sections, green_lesser[0], green_greater[0], coulomb[0], pattern
    )
    polar, screened = screen(results[: 1 + sides], *results[1 + sides :])
    return polar.reshape(1, local, count, 2, width), screened[None]


def solution(mesh):
    in_specs = (
        P("sec", "el", None, None, None),
        P("sec", "el", None, None, None),
        P("sec", None, None, None),
        P(),
    )
    out_specs = (P("sec", "el", None, None, None), P("sec", "el", None, None, None))
    return jax.shard_map(
        functools.partial(on_device, mesh.shape["sec"], mesh.shape["el"]),
        mesh=mesh,
        in_specs=in_specs,
        out_specs=out_specs,
        check_vma=False,
    )
```

```python
import functools

import jax
import jax.numpy as jnp
import numpy as np
from jax import lax
from jax.experimental import pallas as pl
from jax.experimental.pallas import tpu as pltpu
from jax.sharding import PartitionSpec as P

TR = 8
TC = 16
VMEM_LIMIT = 40 * 1024 * 1024
GROUPS = 4
BATCHES = 2
STEPS = 8
LEADS = (1, 1, 3)


def tables(energies):
    length = energies
    depth = energies // 2
    order = np.concatenate([np.arange(0, length, 2), np.arange(1, length, 2)])
    phase = np.outer(order, np.arange(depth)) % length
    phase = phase * (2.0 * np.pi / length)
    cosine = np.cos(phase).astype(np.float32)
    sine = np.sin(phase).astype(np.float32)
    real = np.stack([cosine, sine], axis=2).reshape(length, length)
    imag = np.stack([-sine, cosine], axis=2).reshape(length, length)
    forward = np.concatenate([real, imag], axis=0)
    out_r = np.concatenate([-sine.T, -cosine.T], axis=1)
    out_i = np.concatenate([cosine.T, -sine.T], axis=1)
    inverse = np.stack([out_r, out_i], axis=1).reshape(length, 2 * length)
    return jnp.asarray(forward, jnp.bfloat16), jnp.asarray(inverse, jnp.bfloat16)


def dot32(a, b):
    return jnp.dot(a, b, preferred_element_type=jnp.float32)


def conjugate_product(a, b):
    (ar, ai), (br, bi) = a, b
    return jnp.concatenate([ar * br + ai * bi, ai * br - ar * bi], axis=0).astype(jnp.bfloat16)


def spectra(parts, forward_ref):
    depth, _, width = parts[0].shape
    length = 2 * depth
    joined = jnp.concatenate([p.reshape(length, width) for p in parts], axis=1)
    z = dot32(forward_ref[...], joined)
    return [
        (z[:length, i * width : (i + 1) * width], z[length:, i * width : (i + 1) * width])
        for i in range(len(parts))
    ]


def low_part(factor, lesser, greater, forward_ref, inverse_ref):
    first, second = spectra([lesser, greater], forward_ref)
    return dot32(inverse_ref[...], conjugate_product(first, second)) * factor


def high_parts(factor, lesser, below, greater, forward_ref, inverse_ref):
    width = lesser.shape[-1]
    first, under, second = spectra([lesser, below, greater], forward_ref)
    middle = under[0].shape[0] // 2

    def shifted(a, b):
        return jnp.concatenate([b[:middle] + a[:middle], b[middle:] - a[middle:]], axis=0)

    both = tuple(shifted(a, b) for a, b in zip(under, second))
    product = jnp.concatenate(
        [conjugate_product(first, both), conjugate_product(first, under)], axis=1
    )
    series = dot32(inverse_ref[...], product) * factor
    return series[:, :width], series[:, width:]


def exchange_kernel(
    owners,
    sections,
    factor,
    lesser_ref,
    greater_ref,
    coulomb_ref,
    forward_hbm,
    inverse_hbm,
    pattern_hbm,
    *refs,
):
    sides = 1 if sections == 2 else 2
    polar_ref = refs[0]
    beside_refs = refs[1 : 1 + sides]
    sum_ref, right_ref, picked_last_ref, mask_last_ref, ours_ref = refs[1 + sides : 6 + sides]
    (
        pattern_ref,
        last_ref,
        forward_ref,
        inverse_ref,
        table_sem,
        other_ref,
        coulomb_near,
        picked_ref,
        mask_ref,
        rows_ref,
        near_sem,
        x_ref,
        below_ref,
        down_ref,
        partial_ref,
        d_ref,
        in_send,
        in_recv,
        pass_send,
        pass_recv,
        up_send,
        up_recv,
        down_send,
        down_recv,
        out_send,
        out_recv,
        side_send,
        side_recv,
        c_send,
        c_recv,
    ) = refs[6 + sides :]
    tiles = x_ref.shape[1]
    local = polar_ref.shape[0]
    slots = tiles // GROUPS
    some = local // BATCHES
    group = owners // 4
    half = owners // 2
    me = lax.axis_index("el")
    section = lax.axis_index("sec")
    quarter = me // group
    place = lax.rem(me, group)
    base = quarter * group
    half_base = (quarter // 2) * half
    spot = lax.rem(me, half)
    outer = jnp.logical_or(quarter == 0, quarter == 3)
    inward = jnp.where(quarter == 0, me + group, me - group)
    mesh_id = pl.DeviceIdType.MESH
    if sections == 2:
        targets = [1 - section]
    else:
        targets = [
            lax.rem(section + 1, sections),
            lax.rem(section + sections - 1, sections),
        ]

    load_f = pltpu.make_async_copy(forward_hbm, forward_ref, table_sem.at[0])
    load_i = pltpu.make_async_copy(inverse_hbm, inverse_ref, table_sem.at[1])
    load_p = pltpu.make_async_copy(pattern_hbm, pattern_ref, table_sem.at[2])
    load_f.start()
    load_i.start()
    load_p.start()
    barrier = pltpu.get_barrier_semaphore()

    def greet(step, carry):
        peer = half_base + lax.rem(spot + step, half)
        pl.semaphore_signal(barrier, inc=1, device_id={"el": peer}, device_id_type=mesh_id)
        return carry

    lax.fori_loop(1, half, greet, 0)
    for target in targets:
        pl.semaphore_signal(barrier, inc=1, device_id={"sec": target}, device_id_type=mesh_id)

    @pl.when(quarter < 2)
    def _():
        for peer in range(group):
            pl.semaphore_signal(
                barrier, inc=1, device_id={"el": half + peer}, device_id_type=mesh_id
            )

    @pl.when(quarter == 2)
    def _():
        pl.semaphore_signal(barrier, inc=1, device_id={"el": me - group}, device_id_type=mesh_id)

    greeted = jnp.where(quarter == 2, half, jnp.where(quarter == 1, 1, 0))
    pl.semaphore_wait(barrier, half - 1 + sides + greeted)

    mine = pl.ds(spot * local, local)
    own = pl.ds(lax.rem(quarter, 2) * group * local, group * local)
    theirs = pl.ds((1 - lax.rem(quarter, 2)) * group * local, group * local)

    def send_in(which, source, tile):
        pltpu.make_async_copy(
            source.at[:, place, tile], x_ref.at[which, tile, mine], in_recv.at[which, tile]
        ).start()

        def send(turn, carry):
            peer = lax.rem(place + 1 + turn, group)
            pltpu.make_async_remote_copy(
                src_ref=source.at[:, peer, tile],
                dst_ref=x_ref.at[which, tile, mine],
                send_sem=in_send,
                recv_sem=in_recv.at[which, tile],
                device_id={"el": base + peer},
                device_id_type=mesh_id,
            ).start()
            return carry

        for turn in range(group - 1):
            send(turn, 0)

    def send_both(tile, carry):
        send_in(1, greater_ref, tile)
        send_in(0, lesser_ref, tile)
        return carry

    lax.fori_loop(0, tiles, send_both, 0)

    shared = pltpu.make_async_remote_copy(
        src_ref=coulomb_ref.at[1],
        dst_ref=other_ref,
        send_sem=c_send,
        recv_sem=c_recv,
        device_id={"sec": targets[0]},
        device_id_type=mesh_id,
    )
    shared.start()

    def gathered(which, tile):
        part = x_ref.at[which, tile, own]
        pltpu.make_async_copy(part, part, in_recv.at[which, tile]).wait()

    def pass_inward(which, tile, peer):
        gathered(which, tile)
        pltpu.make_async_remote_copy(
            src_ref=x_ref.at[which, tile, own],
            dst_ref=x_ref.at[which, tile, own],
            send_sem=pass_send,
            recv_sem=pass_recv.at[which, tile],
            device_id={"el": peer},
            device_id_type=mesh_id,
        ).start()

    def passed(which, tile):
        part = x_ref.at[which, tile, theirs]
        pltpu.make_async_copy(part, part, pass_recv.at[which, tile]).wait()

    def forward_copy(tile, side):
        return pltpu.make_async_remote_copy(
            src_ref=polar_ref.at[:, :, tile],
            dst_ref=beside_refs[side].at[:, :, tile],
            send_sem=side_send.at[side, tile],
            recv_sem=side_recv.at[side, tile],
            device_id={"sec": targets[side]},
            device_id_type=mesh_id,
        )

    def pass_on(tile):
        whole = polar_ref.at[:, :, tile]
        pltpu.make_async_copy(whole, whole, out_recv.at[tile]).wait()

        @pl.when(quarter < 2)
        def _():
            part = partial_ref.at[:, :, tile]
            pltpu.make_async_copy(part, part, down_recv.at[tile]).wait()
            both = polar_ref[:, :, tile].astype(jnp.float32)
            both = both + partial_ref[:, :, tile].astype(jnp.float32)
            polar_ref[:, :, tile] = both.astype(jnp.bfloat16)

        for side in range(sides):
            forward_copy(tile, side).start()

    def give(tile):
        pltpu.make_async_copy(
            d_ref.at[tile, mine], polar_ref.at[:, place, tile], out_recv.at[tile]
        ).start()

        def send(turn, carry):
            peer = lax.rem(spot + 1 + turn, half)
            pltpu.make_async_remote_copy(
                src_ref=d_ref.at[tile, pl.ds(peer * local, local)],
                dst_ref=polar_ref.at[:, place, tile],
                send_sem=out_send,
                recv_sem=out_recv.at[tile],
                device_id={"el": half_base + peer},
                device_id_type=mesh_id,
            ).start()
            return carry

        for turn in range(half - 1):
            send(turn, 0)

    def lift(tile):
        gathered(1, tile)
        passed(1, tile)
        pltpu.make_async_remote_copy(
            src_ref=x_ref.at[1, tile],
            dst_ref=below_ref.at[tile],
            send_sem=up_send,
            recv_sem=up_recv.at[tile],
            device_id={"el": me + group},
            device_id_type=mesh_id,
        ).start()
        gathered(0, tile)
        passed(0, tile)
        value = low_part(factor, x_ref[0, tile], x_ref[1, tile], forward_ref, inverse_ref)
        d_ref[tile] = value.astype(jnp.bfloat16).reshape(d_ref.shape[1:])
        give(tile)

    def upper(tile):
        gathered(0, tile)
        gathered(1, tile)
        passed(0, tile)
        passed(1, tile)
        part = below_ref.at[tile]
        pltpu.make_async_copy(part, part, up_recv.at[tile]).wait()
        down, above = high_parts(
            factor, x_ref[0, tile], below_ref[tile], x_ref[1, tile], forward_ref, inverse_ref
        )
        shape = d_ref.shape[1:]
        down_ref[tile] = down.astype(jnp.bfloat16).reshape(shape)
        for peer in range(half):
            pltpu.make_async_remote_copy(
                src_ref=down_ref.at[tile, peer * local : (peer + 1) * local],
                dst_ref=partial_ref.at[:, place, tile],
                send_sem=down_send,
                recv_sem=down_recv.at[tile],
                device_id={"el": peer},
                device_id_type=mesh_id,
            ).start()
        d_ref[tile] = above.astype(jnp.bfloat16).reshape(shape)
        give(tile)

    def prepare():
        pltpu.make_async_copy(coulomb_ref, coulomb_near, near_sem).wait()
        shared.wait_recv()
        screen_setup(
            sections,
            coulomb_near,
            other_ref,
            pattern_ref,
            right_ref,
            picked_ref,
            mask_ref,
            tiles,
        )
        picked_last_ref[...] = picked_ref[GROUPS - 1]
        mask_last_ref[...] = mask_ref[GROUPS - 1]
        for b in range(local):
            sum_ref[b] = jnp.zeros(sum_ref.shape[1:], sum_ref.dtype)

    def screen_some(turn):
        chunk = turn // BATCHES
        batch = lax.rem(turn, BATCHES)

        @pl.when(batch == 0)
        def _():
            for s in range(slots):
                for side in range(sides):
                    forward_copy(chunk * slots + s, side).wait_recv()

        start = batch * some
        columns = pl.ds(chunk * slots, slots)
        sources = [polar_ref, *beside_refs]
        for t in range(1 + sides):
            for b in range(some):
                piece = sources[t][start + b, :, columns]
                rows_ref[t, b] = piece.reshape(rows_ref.shape[2:]).astype(jnp.float32)
        masks = [mask_ref[chunk, t] for t in range(1 + sides)]
        added = screen_chunk(some, rows_ref, masks, right_ref, picked_ref[chunk])
        for b in range(some):
            for c in range(2):
                old = sum_ref[start + b, c].astype(jnp.float32)
                sum_ref[start + b, c] = (old + added[2 * b + c]).astype(jnp.bfloat16)

    pltpu.make_async_copy(coulomb_ref, coulomb_near, near_sem).start()
    load_f.wait()
    load_i.wait()
    load_p.wait()
    turns = (GROUPS - 1) * BATCHES
    stride = max(1, slots // BATCHES)
    behind = 6
    delay = jnp.where(outer, tiles, jnp.where(quarter == 1, behind, 4))
    lead = slots + jnp.where(outer, LEADS[0], jnp.where(quarter == 1, LEADS[1], LEADS[2]))
    last = jnp.maximum(tiles, (turns - 1) * stride + 1 + lead)
    ready = jnp.where(outer, tiles, jnp.where(quarter == 1, 3, 0))

    def body(i, carry):
        @pl.when(jnp.logical_and(outer, i < tiles))
        def _():
            pass_inward(1, i, inward)
            pass_inward(0, i, inward)

        @pl.when(jnp.logical_and(quarter == 1, i < tiles))
        def _():
            lift(i)

        @pl.when(i == ready)
        def _():
            prepare()

        @pl.when(jnp.logical_and(quarter == 2, i < tiles))
        def _():
            upper(i)

        tile = i - delay

        @pl.when(jnp.logical_and(tile >= 0, tile < tiles))
        def _():
            pass_on(tile)

        since = tile - lead
        turn = since // stride

        @pl.when(
            jnp.logical_and(since >= 0, jnp.logical_and(since % stride == 0, turn < turns))
        )
        def _():
            screen_some(turn)

        return carry

    lax.fori_loop(0, last + delay, body, 0)
    for b in range(local):
        piece = polar_ref[b, :, tiles - slots :]
        last_ref[b] = piece.reshape(last_ref.shape[1:]).astype(jnp.float32)
    ours = right_part(local, last_ref, mask_ref[GROUPS - 1, 0], right_ref[0])
    ours_ref[...] = ours.reshape(ours_ref.shape)

    @pl.when(outer)
    def _():
        part = x_ref.at[:, :, own]
        pltpu.make_async_copy(part, part, pass_send).wait()

    @pl.when(jnp.logical_not(outer))
    def _():
        part = d_ref.at[:, pl.ds(0, (half - 1) * local)]
        pltpu.make_async_copy(part, part, out_send).wait()

    @pl.when(quarter == 1)
    def _():
        pltpu.make_async_copy(below_ref, below_ref, up_send).wait()

    @pl.when(quarter == 2)
    def _():
        pltpu.make_async_copy(down_ref, down_ref, down_send).wait()

    part = x_ref.at[:, :, pl.ds(0, (group - 1) * local)]
    pltpu.make_async_copy(part, part, in_send).wait()

    def settle_sent(tile, carry):
        for side in range(sides):
            forward_copy(tile, side).wait_send()
        return carry

    def settle(tile, carry):
        for side in range(sides):
            forward_copy(tile, side).wait()
        return carry

    lax.fori_loop(0, (GROUPS - 1) * slots, settle_sent, 0)
    lax.fori_loop((GROUPS - 1) * slots, tiles, settle, 0)
    shared.wait_send()


def exchange(owners, sections, lesser, greater, coulomb, pattern):
    local, count, _, width = lesser.shape
    group = owners // 4
    tiles = count // group
    energies = local * owners
    depth = energies // 2
    nb = coulomb.shape[1]
    sides = 1 if sections == 2 else 2
    terms = 1 + sides
    chunk = count // GROUPS
    forward, inverse = tables(energies)
    split = (local, group, tiles, 2, width)
    bf16 = jnp.bfloat16
    far = pl.BlockSpec(memory_space=pltpu.HBM)
    near = pl.BlockSpec(memory_space=pltpu.VMEM)
    dma = pltpu.SemaphoreType.DMA
    buffer = pltpu.VMEM((tiles, depth, 2, width), bf16)
    operands = [lesser.reshape(split), greater.reshape(split), coulomb, forward, inverse, pattern]
    return pl.pallas_call(
        functools.partial(exchange_kernel, owners, sections, 1.0 / (energies * energies**0.5)),
        in_specs=[far] * 6,
        out_specs=[near] * (6 + sides),
        out_shape=[pltpu.VMEM(split, bf16)] * (1 + sides)
        + [
            pltpu.VMEM((local, 2, nb, nb), bf16),
            pltpu.VMEM((terms, nb, nb), bf16),
            pltpu.VMEM((nb, terms * TR * chunk), bf16),
            pltpu.VMEM((terms, chunk, nb), bf16),
            pltpu.VMEM((2 * local, TR * chunk, nb), bf16),
        ],
        scratch_shapes=[
            pltpu.VMEM(pattern.shape, pattern.dtype),
            pltpu.VMEM((local, 2 * chunk, width), jnp.float32),
            pltpu.VMEM(forward.shape, bf16),
            pltpu.VMEM(inverse.shape, bf16),
            dma((3,)),
            pltpu.VMEM((nb, nb), bf16),
            pltpu.VMEM(coulomb.shape, bf16),
            pltpu.VMEM((GROUPS, nb, terms * TR * chunk), bf16),
            pltpu.VMEM((GROUPS, terms, chunk, nb), bf16),
            pltpu.VMEM((terms, local // BATCHES, 2 * chunk, width), jnp.float32),
            dma(()),
            pltpu.VMEM((2, tiles, depth, 2, width), bf16),
            buffer,
            buffer,
            pltpu.VMEM(split, bf16),
            buffer,
            dma(()),
            dma((2, tiles)),
            dma(()),
            dma((2, tiles)),
            dma(()),
            dma((tiles,)),
            dma(()),
            dma((tiles,)),
            dma(()),
            dma((tiles,)),
            dma((sides, tiles)),
            dma((sides, tiles)),
            dma(()),
            dma(()),
        ],
        compiler_params=pltpu.CompilerParams(
            collective_id=0, has_side_effects=True, vmem_limit_bytes=VMEM_LIMIT
        ),
    )(*[pltpu.with_memory_space_constraint(array, pltpu.HBM) for array in operands])


def screen_setup(
    sections, coulomb_ref, other_ref, pattern_ref, right_ref, picked_ref, mask_ref, tiles
):
    groups, terms, chunk, nb = mask_ref.shape
    count = groups * chunk
    slots = tiles // groups
    section = lax.axis_index("sec")
    lower = other_ref[...].astype(jnp.float32).T
    upper = coulomb_ref[1].astype(jnp.float32)
    matrices = [coulomb_ref[0].astype(jnp.float32)]
    if sections == 2:
        sources = [section, 1 - section]
        matrices.append(jnp.where(section == 0, upper, lower))
    else:
        sources = [
            section,
            lax.rem(section + sections - 1, sections),
            lax.rem(section + 1, sections),
        ]
        matrices.append(jnp.where(section > 0, lower, 0.0))
        matrices.append(jnp.where(section < sections - 1, upper, 0.0))
    across = nb // TC
    wide = TR * count
    iota = lambda shape, axis: lax.broadcasted_iota(jnp.int32, shape, axis)
    row_of = iota((nb, wide), 0)
    lane = iota((count, wide), 1)
    member = lane % chunk
    listed_at = (member // slots) * tiles + lane // (TR * chunk) * slots + member % slots
    taken = listed_at == iota((count, wide), 0)
    inner_row = iota((1, wide), 1) // chunk % TR
    diagonal = iota((count, count), 0) == iota((count, count), 1)
    member = iota((chunk, count), 0)
    begin = (member // slots) * tiles + member % slots
    column_of = iota((chunk, nb), 1) // TC
    for t in range(terms):
        listed = pattern_ref[pl.ds(sources[t], 1), :].astype(jnp.float32)
        upright = jnp.sum(jnp.where(diagonal, listed, 0.0), axis=1, keepdims=True)
        spread = jnp.sum(jnp.where(taken, upright, 0.0), axis=0, keepdims=True).astype(jnp.int32)
        row = spread // across * TR + inner_row
        chosen = jnp.where(row_of == row, 1.0, 0.0).astype(jnp.bfloat16)
        picked = dot32(matrices[t].astype(jnp.bfloat16), chosen).astype(jnp.bfloat16)
        span = TR * chunk
        for g in range(groups):
            picked_ref[g, :, t * span : (t + 1) * span] = picked[:, g * span : (g + 1) * span]
            here = iota((chunk, count), 1) == begin + g * slots
            place = jnp.sum(jnp.where(here, listed, 0.0), axis=1, keepdims=True).astype(jnp.int32)
            mask_ref[g, t] = jnp.where(column_of == place % across, 1.0, 0.0).astype(jnp.bfloat16)
        right_ref[t] = matrices[t].T.astype(jnp.bfloat16)


def right_part(batch, rows, mask, right):
    chunk, nb = mask.shape
    width = rows.shape[-1]
    lane = lax.broadcasted_iota(jnp.int32, (chunk, width), 1) % TC
    stacked = []
    for b in range(batch):
        for c in range(2):
            tile = rows[b, pl.ds(c, chunk, stride=2), :]
            for r in range(TR):
                spread = jnp.take_along_axis(
                    tile, lane + r * TC, axis=1, mode="promise_in_bounds"
                ).astype(jnp.bfloat16)
                stacked.append(jnp.concatenate([spread] * (nb // width), axis=1) * mask)
    return dot32(jnp.concatenate(stacked, axis=0), right).astype(jnp.bfloat16)


def screen_chunk(batch, rows_ref, masks, right_ref, picked):
    span = TR * masks[0].shape[0]
    halves = [
        right_part(batch, rows_ref.at[t], mask, right_ref[t]) for t, mask in enumerate(masks)
    ]
    added = []
    for n in range(2 * batch):
        part = jnp.concatenate([h[n * span : (n + 1) * span] for h in halves], axis=0)
        added.append(dot32(picked, part))
    return added


def screen_kernel(terms, batch, *refs):
    tile_refs = refs[:terms]
    sum_ref, right_ref, picked_ref, mask_ref, ours_ref, polar_out, out_hbm = refs[terms : terms + 7]
    total_ref, rows_ref, half_ref, keep_sem, total_sem = refs[terms + 7 :]
    polar_ref = tile_refs[0]
    local, _, per, _, _ = polar_ref.shape
    slots = per // GROUPS
    steps = local // batch
    def store(step):
        part = pl.ds(step * batch, batch)
        return pltpu.make_async_copy(total_ref.at[part], out_hbm.at[part], total_sem.at[step])

    keep = pltpu.make_async_copy(polar_ref, polar_out, keep_sem)
    keep.start()
    masks = [mask_ref[t] for t in range(terms)]

    span = TR * mask_ref.shape[1]
    wide = local // max(1, local // 16)

    def fill(step, carry):
        for t in range(1, terms):
            for b in range(wide):
                e = step * wide + b
                piece = tile_refs[t][e, :, per - slots :]
                rows_ref[t, b] = piece.reshape(rows_ref.shape[2:]).astype(jnp.float32)
            half = right_part(wide, rows_ref.at[t], masks[t], right_ref[t])
            half_ref[pl.ds(step * wide * 2, wide * 2), (t - 1) * span : t * span] = half.reshape(
                wide * 2, span, half.shape[-1]
            )
        return carry

    lax.fori_loop(0, local // wide, fill, 0)

    def body(step, carry):
        for b in range(batch):
            for c in range(2):
                e = step * batch + b
                part = jnp.concatenate([ours_ref[2 * e + c], half_ref[2 * e + c]], axis=0)
                total = dot32(picked_ref[...], part)
                total = total + sum_ref[e, c].astype(jnp.float32)
                total_ref[e, c] = total.astype(jnp.bfloat16)
        store(step).start()
        return carry

    for step in range(steps):
        body(step, 0)
    keep.wait()
    for step in range(steps):
        store(step).wait()


def screen(tiles, total, right, picked, mask, ours):
    terms = len(tiles)
    local, _, _, _, width = tiles[0].shape
    chunk = mask.shape[1]
    batch = max(1, local // STEPS)
    dma = pltpu.SemaphoreType.DMA
    return pl.pallas_call(
        functools.partial(screen_kernel, terms, batch),
        in_specs=[pl.BlockSpec(memory_space=pltpu.VMEM)] * (terms + 5),
        out_specs=[pl.BlockSpec(memory_space=pltpu.HBM)] * 2,
        out_shape=[
            jax.ShapeDtypeStruct(tiles[0].shape, jnp.bfloat16),
            jax.ShapeDtypeStruct(total.shape, total.dtype),
        ],
        scratch_shapes=[
            pltpu.VMEM(total.shape, total.dtype),
            pltpu.VMEM((terms, local, 2 * chunk, width), jnp.float32),
            pltpu.VMEM((2 * local, (terms - 1) * TR * chunk, total.shape[-1]), jnp.bfloat16),
            dma(()),
            dma((local // batch,)),
        ],
        compiler_params=pltpu.CompilerParams(vmem_limit_bytes=VMEM_LIMIT),
    )(*tiles, total, right, picked, mask, ours)


def on_device(sections, owners, green_lesser, green_greater, coulomb, pattern):
    _, local, count, _, width = green_lesser.shape
    sides = 1 if sections == 2 else 2
    results = exchange(
        owners, sections, green_lesser[0], green_greater[0], coulomb[0], pattern
    )
    polar, screened = screen(results[: 1 + sides], *results[1 + sides :])
    return polar.reshape(1, local, count, 2, width), screened[None]


def solution(mesh):
    in_specs = (
        P("sec", "el", None, None, None),
        P("sec", "el", None, None, None),
        P("sec", None, None, None),
        P(),
    )
    out_specs = (P("sec", "el", None, None, None), P("sec", "el", None, None, None))
    return jax.shard_map(
        functools.partial(on_device, mesh.shape["sec"], mesh.shape["el"]),
        mesh=mesh,
        in_specs=in_specs,
        out_specs=out_specs,
        check_vma=False,
    )
```
